32 devices in a mesh: scan: 8 (over z, x), tile: 4 (over y, core).
Axes of the slice: x: 2, y: 2, z: 4, core: 2. Of those that a mesh axis runs over, the one named last changes fastest.
Arguments:
- object_slab: float32 [2, 3072, 6144], P(None, 'tile', 'scan'), may hold values from -6 to 6
- probe_field: float32 [2, 512, 512], replicated, may hold values from -3 to 3
- intensities: bfloat16 [8, 4, 6, 512, 512], P('scan', 'tile'), may hold values from 0 to 2
- offsets: int32 [8, 4, 6, 2], P('scan', 'tile'), may hold values from 0 to 767
- live_count: int32 [8, 4], P(None, 'tile'), may hold values from 1 to 6, as said below
Outputs:
- object_grad: float32 [2, 3072, 6144], P(None, 'tile', 'scan')
The draws below stay inside these ranges and needn't reach their ends.
Inputs may be any that keep to these rules, and one draw needn't show every extreme that they name: The first live_count slots of a group hold its measured positions; some group has all 6 slots live.
All inputs are finite; a program needn't handle non-finite values.
Results may differ from the reference program's by a relative error of at most 0.014.
Values may be sent and summed in bfloat16 or wider, within the bound.
A program may use at most 128 MiB of HBM per device.

```python
import math
import jax
import jax.numpy as jnp
from jax import lax

W = 512
TILE = 768
SLOTS = 6
OBJ_Y = 3072
OBJ_X = 6144
N_SCAN = 8
N_TILE = 4


def draw_live_count(key, part):
    key_side, key_high, key_low, key_full = jax.random.split(key, 4)
    shape = (N_SCAN // 2, N_TILE)
    busy_left = jax.random.randint(key_side, shape, 0, 2)
    high = SLOTS - jax.random.randint(key_high, shape, 0, 2)
    low = 1 + jax.random.randint(key_low, shape, 0, max(SLOTS // 4, 1))
    left = jnp.where(busy_left == 1, high, low)
    right = jnp.where(busy_left == 1, low, high)
    counts = jnp.concatenate([left, right], axis=0)
    full_at = jax.random.randint(key_full, (), 0, N_SCAN * N_TILE)
    flat_ids = jnp.arange(N_SCAN * N_TILE, dtype=jnp.int32).reshape((N_SCAN, N_TILE))
    counts = jnp.where(flat_ids == full_at, SLOTS, counts)
    return counts.astype(jnp.int32)


def with_ends(drawn, stream_key, least, largest):
    shape = drawn.shape
    spot = [jax.random.randint(jax.random.fold_in(stream_key, axis), (), 0, shape[axis]) for axis in range(len(shape))]
    drawn = drawn.at[tuple(spot)].set(least)
    longest = shape.index(max(shape))
    spot[longest] = (spot[longest] + 1) % shape[longest]
    return drawn.at[tuple(spot)].set(largest)


def shard_levels(own_key, extent, cuts, low, high):
    def one(position, shards_of):
        draws = jax.random.uniform(jax.random.fold_in(jax.random.fold_in(own_key, 6), position), (shards_of,), jnp.float32, low / len(cuts), high / len(cuts))
        return jnp.repeat(jnp.exp(draws), extent[position] // shards_of).reshape((-1,) + (1,) * (len(extent) - position - 1))

    gain = one(*cuts[0])
    for cut in cuts[1:]:
        gain = gain * one(*cut)
    return gain


def normal_values(own_key, extent, width, most, pieces=(), held_as=jnp.bfloat16):
    result = width * jax.random.normal(own_key, extent, jnp.float32)
    if pieces:
        result = result * shard_levels(own_key, extent, pieces, -0.22, 0.18)
    return jnp.clip(result, -most, most).astype(held_as)


def setup_inputs(seed: int = 0) -> dict:
    arg_keys = jax.random.split(jax.random.key(seed), 6)
    return {
        "object_slab": normal_values(arg_keys[0], (2, OBJ_Y, OBJ_X), 1.0, 6.0, ((1, 4), (2, 8)), jnp.float32),
        "probe_field": normal_values(arg_keys[1], (2, W, W), 0.5, 3.0, (), jnp.float32),
        "intensities": jnp.clip(2.0 * jax.random.uniform(arg_keys[2], (N_SCAN, N_TILE, SLOTS, W, W), jnp.float32) ** shard_levels(arg_keys[2], (N_SCAN, N_TILE, SLOTS, W, W), ((0, 8), (1, 4)), -0.2, 0.2), 0.0, 2.0).astype(jnp.bfloat16),
        "offsets": with_ends(jax.random.randint(arg_keys[3], (N_SCAN, N_TILE, SLOTS, 2), 0, TILE), jax.random.fold_in(arg_keys[3], 1), 0, TILE - 1).astype(jnp.int32),
        "live_count": draw_live_count(jax.random.fold_in(arg_keys[5], 71), 0),
    }


def fourier_tables(side_len):
    across = jnp.arange(side_len, dtype=jnp.int32)
    phase = (across[:, None] * across[None, :] % side_len).astype(jnp.float32) * (2.0 * math.pi / side_len)
    factor = 1.0 / math.sqrt(side_len)
    return ((jnp.cos(phase) * factor).astype(jnp.bfloat16), (-jnp.sin(phase) * factor).astype(jnp.bfloat16))

def left_apply(table_re, table_im, part_re, part_im):
    side_len = part_re.shape[-1]
    joined = jnp.concatenate([part_re, part_im], axis=-1).astype(jnp.float32)
    with_re = jnp.einsum('ij,bjk->bik', table_re.astype(jnp.float32), joined)
    with_im = jnp.einsum('ij,bjk->bik', table_im.astype(jnp.float32), joined)
    return (with_re[..., :side_len] - with_im[..., side_len:], with_re[..., side_len:] + with_im[..., :side_len])

def right_apply(part_re, part_im, table_re, table_im):
    side_len = part_re.shape[-1]
    joined = jnp.concatenate([part_re, part_im], axis=-2).astype(jnp.float32)
    with_re = jnp.einsum('bij,jk->bik', joined, table_re.astype(jnp.float32))
    with_im = jnp.einsum('bij,jk->bik', joined, table_im.astype(jnp.float32))
    return (with_re[:, :side_len] - with_im[:, side_len:], with_im[:, :side_len] + with_re[:, side_len:])

def transform(exit_waves, measured, tables):
    table_re, table_im = tables
    conj_im = -table_im
    half_re, half_im = left_apply(table_re, table_im, exit_waves[:, 0], exit_waves[:, 1])
    half_re = half_re.astype(jnp.bfloat16)
    half_im = half_im.astype(jnp.bfloat16)
    far_re, far_im = right_apply(half_re, half_im, table_re, table_im)
    misfit = far_re * far_re + far_im * far_im - measured.astype(jnp.float32)
    mis_re = (misfit * far_re).astype(jnp.bfloat16)
    mis_im = (misfit * far_im).astype(jnp.bfloat16)
    back_re, back_im = left_apply(table_re, conj_im, mis_re, mis_im)
    back_re = back_re.astype(jnp.bfloat16)
    back_im = back_im.astype(jnp.bfloat16)
    grad_re, grad_im = right_apply(back_re, back_im, table_re, conj_im)
    return jnp.stack([grad_re, grad_im], axis=1).astype(jnp.bfloat16)

def exit_wave(probe_field, patches):
    probe_re = probe_field[0]
    probe_im = probe_field[1]
    real_part = probe_re * patches[:, 0] - probe_im * patches[:, 1]
    imag_part = probe_re * patches[:, 1] + probe_im * patches[:, 0]
    return jnp.stack([real_part, imag_part], axis=1).astype(jnp.bfloat16)

def object_gradient(probe_field, wave_grads):
    probe_re = probe_field[0]
    probe_im = probe_field[1]
    grad_re = wave_grads[:, 0].astype(jnp.float32)
    grad_im = wave_grads[:, 1].astype(jnp.float32)
    real_part = probe_re * grad_re + probe_im * grad_im
    imag_part = probe_re * grad_im - probe_im * grad_re
    return jnp.stack([real_part, imag_part], axis=1)

def reference(object_slab, probe_field, intensities, offsets, live_count):
    side_len = probe_field.shape[-1]
    grid_rows = object_slab.shape[1]
    grid_cols = object_slab.shape[2]
    padded = jnp.pad(object_slab, ((0, 0), (0, side_len), (0, side_len)))
    groups = N_SCAN * N_TILE
    flat_measured = intensities.reshape(groups, SLOTS, side_len, side_len)
    flat_shifts = offsets.reshape(groups, SLOTS, 2)
    flat_live = live_count.reshape(groups)
    group_ids = jnp.arange(groups, dtype=jnp.int32)
    scan_ids = group_ids // N_TILE
    tile_ids = group_ids % N_TILE
    zero_index = jnp.zeros((), jnp.int32)
    tables = fourier_tables(side_len)

    def one_group(gradient_sum, inputs):
        measured, shifts, live_total, scan_id, tile_id = inputs
        row_start = (tile_id * TILE + shifts[:, 0]).astype(jnp.int32)
        col_start = (scan_id * TILE + shifts[:, 1]).astype(jnp.int32)

        def cut_patch(row_at, col_at):
            return lax.dynamic_slice(padded, (zero_index, row_at, col_at), (2, side_len, side_len))
        patches = jax.vmap(cut_patch)(row_start, col_start)
        exit_waves = exit_wave(probe_field, patches)
        wave_grads = transform(exit_waves, measured, tables)
        live_mask = (jnp.arange(SLOTS, dtype=jnp.int32) < live_total).astype(jnp.float32)
        patch_grad = object_gradient(probe_field, wave_grads) * live_mask[:, None, None, None]

        def add_one(slot_index, running):
            corner = (zero_index, row_start[slot_index], col_start[slot_index])
            current = lax.dynamic_slice(running, corner, (2, side_len, side_len))
            return lax.dynamic_update_slice(running, current + patch_grad[slot_index], corner)
        return (lax.fori_loop(0, SLOTS, add_one, gradient_sum), None)
    gradient_sum = jnp.zeros(padded.shape, jnp.float32)
    gradient_sum, unused = lax.scan(one_group, gradient_sum, (flat_measured, flat_shifts, flat_live, scan_ids, tile_ids))
    return gradient_sum[:, :grid_rows, :grid_cols]
```

```python
import functools
import math

import jax
import jax.numpy as jnp
from jax import lax
from jax.experimental import pallas as pl
from jax.experimental.pallas import tpu as pltpu
from jax.sharding import PartitionSpec as P

RADIX = 4
LANES = 128


def from_behind(value, axis, by):
    peers = lax.axis_size(axis)
    pairs = [(i, i + by) for i in range(peers) if 0 <= i + by < peers]
    return lax.ppermute(value, axis, pairs)


def residue_tables(side_len):
    part = side_len // RADIX
    freq = jnp.arange(side_len, dtype=jnp.int32).reshape(part, RADIX).T
    across = jnp.arange(part, dtype=jnp.int32)
    phase = (freq[:, :, None] * across[None, None, :] % side_len).astype(jnp.float32) * (
        2.0 * math.pi / side_len
    )
    factor = 1.0 / math.sqrt(side_len)
    cos = (jnp.cos(phase) * factor).astype(jnp.bfloat16)
    sin = (jnp.sin(phase) * factor).astype(jnp.bfloat16)
    rows = jnp.concatenate(
        [jnp.concatenate([cos, sin], axis=2), jnp.concatenate([-sin, cos], axis=2)], axis=1
    )
    return rows, jnp.swapaxes(rows, 1, 2)


def sorted_by_residue(side_len):
    at = jnp.arange(side_len, dtype=jnp.int32)
    source = at % (side_len // RADIX) * RADIX + at // (side_len // RADIX)
    return (source[:, None] == at[None, :]).astype(jnp.bfloat16)


def dot(a, b):
    return jnp.dot(a, b, preferred_element_type=jnp.float32)


def butterfly(parts, sign):
    (r0, i0), (r1, i1), (r2, i2), (r3, i3) = parts
    ar, ai, br, bi = r0 + r2, i0 + i2, r1 + r3, i1 + i3
    cr, ci, dr, di = r0 - r2, i0 - i2, r1 - r3, i1 - i3
    plus = (cr - di, ci + dr)
    minus = (cr + di, ci - dr)
    first, third = (plus, minus) if sign > 0 else (minus, plus)
    return [(ar + br, ai + bi), first, (ar - br, ai - bi), third]


def sort_kernel(sort_ref, unsort_ref, measured_ref, out_ref):
    rows = dot(sort_ref[...], measured_ref[0]).astype(jnp.bfloat16)
    out_ref[0] = dot(rows, unsort_ref[...]).astype(jnp.bfloat16)


def sort_measured(measured):
    slots, side_len, _ = measured.shape
    sort = sorted_by_residue(side_len)
    whole = pl.BlockSpec((side_len, side_len), lambda i: (0, 0))
    block = pl.BlockSpec((1, side_len, side_len), lambda i: (i, 0, 0))
    return pl.pallas_call(
        sort_kernel,
        grid=(slots,),
        out_shape=jax.ShapeDtypeStruct(measured.shape, jnp.bfloat16),
        in_specs=[whole, whole, block],
        out_specs=block,
        cost_estimate=pl.CostEstimate(
            flops=4 * slots * side_len**3, bytes_accessed=4 * measured.size, transcendentals=0
        ),
    )(sort, sort.T, measured)


def solve_kernel(
    live_ref,
    shift_ref,
    own_ref,
    right_ref,
    below_ref,
    corner_ref,
    probe_ref,
    measured_ref,
    rows_ref,
    cols_ref,
    out_ref,
    out_right_ref,
    out_below_ref,
    out_corner_ref,
    field,
    grown,
    mixed,
    spectra,
    backs,
):
    tile_len = own_ref.shape[1]
    side_len = probe_ref.shape[1]
    part = side_len // RADIX
    own_blocks = tile_len // LANES
    side_blocks = side_len // LANES
    lane = lax.broadcasted_iota(jnp.int32, (1, LANES), 1)

    for c in range(2):
        for b in range(own_blocks):
            at = slice(b * LANES, (b + 1) * LANES)
            field[c, b, :tile_len, :] = own_ref[c, :, at]
            field[c, b, tile_len:, :] = below_ref[c, :, at].astype(jnp.float32)
        for b in range(side_blocks):
            at = slice(b * LANES, (b + 1) * LANES)
            field[c, own_blocks + b, :tile_len, :] = right_ref[c, :, at].astype(jnp.float32)
            field[c, own_blocks + b, tile_len:, :] = corner_ref[c, :, at].astype(jnp.float32)
    grown[...] = jnp.zeros_like(grown)

    def one_slot(slot, carry):
        row = shift_ref[slot, 0]
        col = shift_ref[slot, 1]
        block = lax.div(col, LANES)
        turn = lax.rem(col, LANES)
        back_turn = lax.rem(LANES - turn, LANES)
        keep = lane < LANES - turn
        enter = lane >= turn
        height = 16

        def load_rows(i, carry):
            at = pl.multiple_of(i * height, height)
            waves = []
            for p in range(RADIX):
                cuts = []
                for c in range(2):
                    turned = [
                        pltpu.roll(
                            field[c, block + b, pl.ds(row + at + p * part, height), :], back_turn, 1
                        )
                        for b in range(side_blocks + 1)
                    ]
                    cuts.append(
                        [jnp.where(keep, turned[b], turned[b + 1]) for b in range(side_blocks)]
                    )
                blocks = []
                for b in range(side_blocks):
                    cols = slice(b * LANES, (b + 1) * LANES)
                    probe_re = probe_ref[0, pl.ds(at + p * part, height), cols]
                    probe_im = probe_ref[1, pl.ds(at + p * part, height), cols]
                    re, im = cuts[0][b], cuts[1][b]
                    blocks.append((probe_re * re - probe_im * im, probe_re * im + probe_im * re))
                waves.append(blocks)
            for b in range(side_blocks):
                cols = slice(b * LANES, (b + 1) * LANES)
                sums = butterfly([waves[p][b] for p in range(RADIX)], -1)
                for q in range(RADIX):
                    mixed[q, pl.ds(at, height), cols] = sums[q][0].astype(jnp.bfloat16)
                    mixed[q, pl.ds(at + part, height), cols] = sums[q][1].astype(jnp.bfloat16)
            return carry

        lax.fori_loop(0, part // height, load_rows, 0)

        for q in range(RADIX):
            half = dot(rows_ref[q], mixed[q])
            parts = [
                (half[:part, p * part : (p + 1) * part], half[part:, p * part : (p + 1) * part])
                for p in range(RADIX)
            ]
            misfits = []
            for other, (re, im) in enumerate(butterfly(parts, -1)):
                far = dot(jnp.concatenate([re, im], axis=1).astype(jnp.bfloat16), cols_ref[other])
                far_re, far_im = far[:, :part], far[:, part:]
                seen = measured_ref[
                    slot, q * part : (q + 1) * part, other * part : (other + 1) * part
                ].astype(jnp.float32)
                misfit = far_re * far_re + far_im * far_im - seen
                misfits.append(
                    jnp.concatenate([misfit * far_re, misfit * far_im], axis=0).astype(jnp.bfloat16)
                )
            spectra[q] = dot(cols_ref[q], jnp.concatenate(misfits, axis=1))

        def mix_rows(i, carry):
            at = pl.multiple_of(i * height, height)
            for other in range(RADIX):
                cols = slice(other * part, (other + 1) * part)
                parts = [
                    (spectra[q, pl.ds(at, height), cols], spectra[q, pl.ds(at + part, height), cols])
                    for q in range(RADIX)
                ]
                for p, (re, im) in enumerate(butterfly(parts, 1)):
                    backs[other, pl.ds(at + p * part, height), :] = jnp.concatenate(
                        [re, im], axis=1
                    ).astype(jnp.bfloat16)
            return carry

        lax.fori_loop(0, part // height, mix_rows, 0)

        def add_rows(i, carry):
            tall = 64
            at = pl.multiple_of(i * tall, tall)
            parts = []
            for other in range(RADIX):
                grad = dot(backs[other, pl.ds(at, tall), :], rows_ref[other])
                parts.append((grad[:, :part], grad[:, part:]))
            turned = [[], []]
            for b, (re, im) in enumerate(butterfly(parts, 1)):
                cols = slice(b * part, (b + 1) * part)
                probe_re = probe_ref[0, pl.ds(at, tall), cols]
                probe_im = probe_ref[1, pl.ds(at, tall), cols]
                turned[0].append(pltpu.roll(probe_re * re + probe_im * im, turn, 1))
                turned[1].append(pltpu.roll(probe_re * im - probe_im * re, turn, 1))
            for c in range(2):
                for b in range(side_blocks + 1):
                    if b == 0:
                        value = jnp.where(enter, turned[c][0], 0.0)
                    elif b == side_blocks:
                        value = jnp.where(enter, 0.0, turned[c][b - 1])
                    else:
                        value = jnp.where(enter, turned[c][b], turned[c][b - 1])
                    grown[c, block + b, pl.ds(row + at, tall), :] += value
            return carry

        lax.fori_loop(0, side_len // 64, add_rows, 0)
        return carry

    lax.fori_loop(0, live_ref[0], one_slot, 0)

    for c in range(2):
        for b in range(own_blocks):
            at = slice(b * LANES, (b + 1) * LANES)
            out_ref[c, :, at] = grown[c, b, :tile_len, :]
            out_below_ref[c, :, at] = grown[c, b, tile_len:, :].astype(jnp.bfloat16)
        for b in range(side_blocks):
            at = slice(b * LANES, (b + 1) * LANES)
            out_right_ref[c, :, at] = grown[c, own_blocks + b, :tile_len, :].astype(jnp.bfloat16)
            out_corner_ref[c, :, at] = grown[c, own_blocks + b, tile_len:, :].astype(jnp.bfloat16)


def solve(live_total, shifts, own, right, below, corner, probe, measured, tables):
    tile_len = own.shape[1]
    side_len = probe.shape[1]
    blocks = (tile_len + side_len) // LANES
    smem = pl.BlockSpec(memory_space=pltpu.SMEM)
    vmem = pl.BlockSpec(memory_space=pltpu.VMEM)
    part = side_len // RADIX
    return pl.pallas_call(
        solve_kernel,
        out_shape=[
            jax.ShapeDtypeStruct(own.shape, jnp.float32),
            jax.ShapeDtypeStruct(right.shape, jnp.bfloat16),
            jax.ShapeDtypeStruct(below.shape, jnp.bfloat16),
            jax.ShapeDtypeStruct(corner.shape, jnp.bfloat16),
        ],
        in_specs=[smem, smem] + [vmem] * 8,
        out_specs=[vmem] * 4,
        scratch_shapes=[
            pltpu.VMEM((2, blocks, tile_len + side_len, LANES), jnp.float32),
            pltpu.VMEM((2, blocks, tile_len + side_len, LANES), jnp.float32),
            pltpu.VMEM((RADIX, 2 * part, side_len), jnp.bfloat16),
            pltpu.VMEM((RADIX, 2 * part, side_len), jnp.float32),
            pltpu.VMEM((RADIX, side_len, 2 * part), jnp.bfloat16),
        ],
        compiler_params=pltpu.CompilerParams(vmem_limit_bytes=60 * 1024 * 1024),
    )(live_total, shifts, own, right, below, corner, probe, measured, *tables)


def shards(object_slab, probe_field, intensities, offsets, live_count):
    side_len = probe_field.shape[-1]
    tile_len = object_slab.shape[1]
    sent = object_slab.astype(jnp.bfloat16)
    right = from_behind(sent[:, :, :side_len], "scan", -1)
    below = from_behind(sent[:, :side_len, :], "tile", -1)
    corner = from_behind(right[:, :side_len, :], "tile", -1)
    tables = residue_tables(side_len)
    measured = sort_measured(intensities[0, 0])
    live_total = live_count[lax.axis_index("scan")]
    own, spill, dropped, both = solve(
        live_total, offsets[0, 0], object_slab, right, below, corner, probe_field, measured, tables
    )
    both = from_behind(both, "tile", 1)
    dropped = from_behind(dropped, "tile", 1)
    upper = spill[:, :side_len, :].astype(jnp.float32) + both.astype(jnp.float32)
    lower = from_behind(spill[:, side_len:, :], "scan", 1)
    upper = from_behind(upper.astype(jnp.bfloat16), "scan", 1)
    spill = jnp.concatenate([upper, lower], axis=1).astype(jnp.float32)
    rest = tile_len - side_len
    return (
        own
        + jnp.pad(spill, ((0, 0), (0, 0), (0, rest)))
        + jnp.pad(dropped.astype(jnp.float32), ((0, 0), (0, rest), (0, 0)))
    )


def solution(mesh):
    placed = (
        P(None, "tile", "scan"),
        P(),
        P("scan", "tile", None, None, None),
        P("scan", "tile", None, None),
        P(None, "tile"),
    )
    return jax.shard_map(
        shards, mesh=mesh, in_specs=placed, out_specs=P(None, "tile", "scan"), check_vma=False
    )
```

```python
import functools
import math

import jax
import jax.numpy as jnp
import numpy as np
from jax import lax
from jax.experimental import pallas as pl
from jax.experimental.pallas import tpu as pltpu
from jax.sharding import PartitionSpec as P

RADIX = 4
LANES = 128


def residue_tables(side_len):
    part = side_len // RADIX
    freq = np.arange(side_len).reshape(part, RADIX).T
    across = np.arange(part)
    phase = (freq[:, :, None] * across[None, None, :] % side_len) * (2.0 * math.pi / side_len)
    factor = 1.0 / math.sqrt(side_len)
    cos = np.cos(phase) * factor
    sin = np.sin(phase) * factor
    rows = np.concatenate(
        [np.concatenate([cos, sin], axis=2), np.concatenate([-sin, cos], axis=2)], axis=1
    ).astype(np.float32)
    return jnp.asarray(rows, jnp.bfloat16), jnp.asarray(rows.swapaxes(1, 2), jnp.bfloat16)


def sorted_by_residue(side_len):
    at = np.arange(side_len)
    source = at % (side_len // RADIX) * RADIX + at // (side_len // RADIX)
    sort = (source[:, None] == at[None, :]).astype(np.float32)
    return jnp.asarray(sort, jnp.bfloat16), jnp.asarray(sort.T, jnp.bfloat16)


def dot(a, b):
    return jnp.dot(a, b, preferred_element_type=jnp.float32)


def butterfly(parts, sign):
    (r0, i0), (r1, i1), (r2, i2), (r3, i3) = parts
    ar, ai, br, bi = r0 + r2, i0 + i2, r1 + r3, i1 + i3
    cr, ci, dr, di = r0 - r2, i0 - i2, r1 - r3, i1 - i3
    plus = (cr - di, ci + dr)
    minus = (cr + di, ci - dr)
    first, third = (plus, minus) if sign > 0 else (minus, plus)
    return [(ar + br, ai + bi), first, (ar - br, ai - bi), third]


def neighbours(axes):
    result = []
    for name, count in axes:
        me = lax.axis_index(name)
        result.append((me > 0, {name: me - 1}, me < count - 1, {name: me + 1}))
    return result


def meet(peers):
    barrier = pltpu.get_barrier_semaphore()
    for has_low, low, has_high, high in peers:
        for there, peer in ((has_low, low), (has_high, high)):

            @pl.when(there)
            def _(peer=peer):
                pl.semaphore_signal(
                    barrier, inc=1, device_id=peer, device_id_type=pl.DeviceIdType.MESH
                )

    count = sum(
        there.astype(jnp.int32) for has_low, _, has_high, _ in peers for there in (has_low, has_high)
    )
    pl.semaphore_wait(barrier, count)


def remote(source, target, sends, receives, index, peer):
    return pltpu.make_async_remote_copy(
        src_ref=source,
        dst_ref=target,
        send_sem=sends.at[index],
        recv_sem=receives.at[index],
        device_id=peer,
        device_id_type=pl.DeviceIdType.MESH,
    )


def gather_kernel(
    axes,
    own_ref,
    measured_ref,
    sort_ref,
    unsort_ref,
    right_ref,
    below_ref,
    corner_ref,
    sorted_ref,
    sent,
    sends,
    receives,
):
    side_len = measured_ref.shape[-1]
    scan, tile = neighbours(axes)
    has_left, left, has_right, _ = scan
    has_up, up, has_down, _ = tile
    sent[:, :side_len, :] = own_ref[:, :side_len, :].astype(jnp.bfloat16)
    sent[:, side_len:, :side_len] = own_ref[:, side_len:, :side_len].astype(jnp.bfloat16)
    meet((scan, tile))
    top = remote(
        sent.at[:, :side_len, :side_len], right_ref.at[:, :side_len, :], sends, receives, 0, left
    )
    rest = remote(
        sent.at[:, side_len:, :side_len], right_ref.at[:, side_len:, :], sends, receives, 1, left
    )
    under = remote(sent.at[:, :side_len, :], below_ref, sends, receives, 2, up)
    corner = remote(right_ref.at[:, :side_len, :], corner_ref, sends, receives, 3, up)

    @pl.when(has_left)
    def _():
        top.start()
        rest.start()

    @pl.when(has_up)
    def _():
        under.start()

    @pl.when(jnp.logical_not(has_right))
    def _():
        right_ref[...] = jnp.zeros_like(right_ref)

    @pl.when(jnp.logical_not(has_down))
    def _():
        below_ref[...] = jnp.zeros_like(below_ref)
        corner_ref[...] = jnp.zeros_like(corner_ref)

    def sort_slot(slot, carry):
        rows = dot(sort_ref[...], measured_ref[slot]).astype(jnp.bfloat16)
        sorted_ref[slot] = dot(rows, unsort_ref[...]).astype(jnp.bfloat16)
        return carry

    lax.fori_loop(0, measured_ref.shape[0], sort_slot, 0)

    @pl.when(has_right)
    def _():
        top.wait_recv()

    @pl.when(has_up)
    def _():
        corner.start()

    @pl.when(has_right)
    def _():
        rest.wait_recv()

    @pl.when(has_down)
    def _():
        under.wait_recv()
        corner.wait_recv()

    @pl.when(has_left)
    def _():
        top.wait_send()
        rest.wait_send()

    @pl.when(has_up)
    def _():
        under.wait_send()
        corner.wait_send()


def gather(axes, own, measured):
    side_len = measured.shape[-1]
    tile_len = own.shape[1]
    vmem = pl.BlockSpec(memory_space=pltpu.VMEM)
    return pl.pallas_call(
        functools.partial(gather_kernel, axes),
        out_shape=[
            jax.ShapeDtypeStruct((2, tile_len, side_len), jnp.bfloat16),
            jax.ShapeDtypeStruct((2, side_len, tile_len), jnp.bfloat16),
            jax.ShapeDtypeStruct((2, side_len, side_len), jnp.bfloat16),
            jax.ShapeDtypeStruct(measured.shape, jnp.bfloat16),
        ],
        in_specs=[vmem] * 4,
        out_specs=[vmem] * 4,
        scratch_shapes=[
            pltpu.VMEM((2, tile_len, tile_len), jnp.bfloat16),
            pltpu.SemaphoreType.DMA((4,)),
            pltpu.SemaphoreType.DMA((4,)),
        ],
        compiler_params=pltpu.CompilerParams(
            collective_id=0, has_side_effects=True, vmem_limit_bytes=40 * 1024 * 1024
        ),
    )(own, measured, *sorted_by_residue(side_len))


def scatter_kernel(
    axes,
    spill_ref,
    drop_ref,
    both_ref,
    from_left_ref,
    from_up_ref,
    joined,
    landed,
    sends,
    receives,
):
    side_len = both_ref.shape[1]
    scan, tile = neighbours(axes)
    has_left, _, has_right, right = scan
    has_up, _, has_down, down = tile
    meet((scan, tile))
    corner = remote(both_ref, landed, sends, receives, 0, down)
    under = remote(drop_ref, from_up_ref, sends, receives, 1, down)
    rest = remote(
        spill_ref.at[:, side_len:, :], from_left_ref.at[:, side_len:, :], sends, receives, 2, right
    )
    top = remote(joined, from_left_ref.at[:, :side_len, :], sends, receives, 3, right)

    @pl.when(has_down)
    def _():
        corner.start()

    @pl.when(has_right)
    def _():
        rest.start()

    @pl.when(has_down)
    def _():
        under.start()

    @pl.when(jnp.logical_not(has_left))
    def _():
        from_left_ref[...] = jnp.zeros_like(from_left_ref)

    @pl.when(jnp.logical_not(has_up))
    def _():
        from_up_ref[...] = jnp.zeros_like(from_up_ref)
        landed[...] = jnp.zeros_like(landed)

    @pl.when(has_up)
    def _():
        corner.wait_recv()

    joined[...] = (
        spill_ref[:, :side_len, :].astype(jnp.float32) + landed[...].astype(jnp.float32)
    ).astype(jnp.bfloat16)

    @pl.when(has_right)
    def _():
        top.start()

    @pl.when(has_left)
    def _():
        rest.wait_recv()
        top.wait_recv()

    @pl.when(has_up)
    def _():
        under.wait_recv()

    @pl.when(has_right)
    def _():
        rest.wait_send()
        top.wait_send()

    @pl.when(has_down)
    def _():
        corner.wait_send()
        under.wait_send()


def scatter(axes, spill, dropped, both):
    vmem = pl.BlockSpec(memory_space=pltpu.VMEM)
    return pl.pallas_call(
        functools.partial(scatter_kernel, axes),
        out_shape=[
            jax.ShapeDtypeStruct(spill.shape, jnp.bfloat16),
            jax.ShapeDtypeStruct(dropped.shape, jnp.bfloat16),
        ],
        in_specs=[vmem] * 3,
        out_specs=[vmem] * 2,
        scratch_shapes=[
            pltpu.VMEM(both.shape, jnp.bfloat16),
            pltpu.VMEM(both.shape, jnp.bfloat16),
            pltpu.SemaphoreType.DMA((4,)),
            pltpu.SemaphoreType.DMA((4,)),
        ],
        compiler_params=pltpu.CompilerParams(
            collective_id=1, has_side_effects=True, vmem_limit_bytes=30 * 1024 * 1024
        ),
    )(spill, dropped, both)


def solve_kernel(
    live_ref,
    shift_ref,
    own_ref,
    right_ref,
    below_ref,
    corner_ref,
    probe_ref,
    measured_ref,
    rows_ref,
    cols_ref,
    out_ref,
    out_right_ref,
    out_below_ref,
    out_corner_ref,
    field,
    grown,
    mixed,
    spectra,
    backs,
):
    tile_len = own_ref.shape[1]
    side_len = probe_ref.shape[1]
    part = side_len // RADIX
    own_blocks = tile_len // LANES
    side_blocks = side_len // LANES
    lane = lax.broadcasted_iota(jnp.int32, (1, LANES), 1)

    for c in range(2):
        for b in range(own_blocks):
            at = slice(b * LANES, (b + 1) * LANES)
            field[c, b, :tile_len, :] = own_ref[c, :, at]
            field[c, b, tile_len:, :] = below_ref[c, :, at].astype(jnp.float32)
        for b in range(side_blocks):
            at = slice(b * LANES, (b + 1) * LANES)
            field[c, own_blocks + b, :tile_len, :] = right_ref[c, :, at].astype(jnp.float32)
            field[c, own_blocks + b, tile_len:, :] = corner_ref[c, :, at].astype(jnp.float32)
    grown[...] = jnp.zeros_like(grown)

    def one_slot(slot, carry):
        row = shift_ref[slot, 0]
        col = shift_ref[slot, 1]
        block = lax.div(col, LANES)
        turn = lax.rem(col, LANES)
        back_turn = lax.rem(LANES - turn, LANES)
        keep = lane < LANES - turn
        enter = lane >= turn
        height = 16

        def load_rows(i, carry):
            at = pl.multiple_of(i * height, height)
            waves = []
            for p in range(RADIX):
                cuts = []
                for c in range(2):
                    turned = [
                        pltpu.roll(
                            field[c, block + b, pl.ds(row + at + p * part, height), :], back_turn, 1
                        )
                        for b in range(side_blocks + 1)
                    ]
                    cuts.append(
                        [jnp.where(keep, turned[b], turned[b + 1]) for b in range(side_blocks)]
                    )
                blocks = []
                for b in range(side_blocks):
                    cols = slice(b * LANES, (b + 1) * LANES)
                    probe_re = probe_ref[0, pl.ds(at + p * part, height), cols]
                    probe_im = probe_ref[1, pl.ds(at + p * part, height), cols]
                    re, im = cuts[0][b], cuts[1][b]
                    blocks.append((probe_re * re - probe_im * im, probe_re * im + probe_im * re))
                waves.append(blocks)
            for b in range(side_blocks):
                cols = slice(b * LANES, (b + 1) * LANES)
                sums = butterfly([waves[p][b] for p in range(RADIX)], -1)
                for q in range(RADIX):
                    mixed[q, pl.ds(at, height), cols] = sums[q][0].astype(jnp.bfloat16)
                    mixed[q, pl.ds(at + part, height), cols] = sums[q][1].astype(jnp.bfloat16)
            return carry

        lax.fori_loop(0, part // height, load_rows, 0)

        for q in range(RADIX):
            half = dot(rows_ref[q], mixed[q])
            parts = [
                (half[:part, p * part : (p + 1) * part], half[part:, p * part : (p + 1) * part])
                for p in range(RADIX)
            ]
            misfits = []
            for other, (re, im) in enumerate(butterfly(parts, -1)):
                far = dot(jnp.concatenate([re, im], axis=1).astype(jnp.bfloat16), cols_ref[other])
                far_re, far_im = far[:, :part], far[:, part:]
                seen = measured_ref[
                    slot, q * part : (q + 1) * part, other * part : (other + 1) * part
                ].astype(jnp.float32)
                misfit = far_re * far_re + far_im * far_im - seen
                misfits.append(
                    jnp.concatenate([misfit * far_re, misfit * far_im], axis=0).astype(jnp.bfloat16)
                )
            spectra[q] = dot(cols_ref[q], jnp.concatenate(misfits, axis=1))

        def mix_rows(i, carry):
            at = pl.multiple_of(i * height, height)
            for other in range(RADIX):
                cols = slice(other * part, (other + 1) * part)
                parts = [
                    (spectra[q, pl.ds(at, height), cols], spectra[q, pl.ds(at + part, height), cols])
                    for q in range(RADIX)
                ]
                for p, (re, im) in enumerate(butterfly(parts, 1)):
                    backs[other, pl.ds(at + p * part, height), :] = jnp.concatenate(
                        [re, im], axis=1
                    ).astype(jnp.bfloat16)
            return carry

        lax.fori_loop(0, part // height, mix_rows, 0)

        def add_rows(i, carry):
            tall = 64
            at = pl.multiple_of(i * tall, tall)
            parts = []
            for other in range(RADIX):
                grad = dot(backs[other, pl.ds(at, tall), :], rows_ref[other])
                parts.append((grad[:, :part], grad[:, part:]))
            turned = [[], []]
            for b, (re, im) in enumerate(butterfly(parts, 1)):
                cols = slice(b * part, (b + 1) * part)
                probe_re = probe_ref[0, pl.ds(at, tall), cols]
                probe_im = probe_ref[1, pl.ds(at, tall), cols]
                turned[0].append(pltpu.roll(probe_re * re + probe_im * im, turn, 1))
                turned[1].append(pltpu.roll(probe_re * im - probe_im * re, turn, 1))
            for c in range(2):
                for b in range(side_blocks + 1):
                    if b == 0:
                        value = jnp.where(enter, turned[c][0], 0.0)
                    elif b == side_blocks:
                        value = jnp.where(enter, 0.0, turned[c][b - 1])
                    else:
                        value = jnp.where(enter, turned[c][b], turned[c][b - 1])
                    grown[c, block + b, pl.ds(row + at, tall), :] += value
            return carry

        lax.fori_loop(0, side_len // 64, add_rows, 0)
        return carry

    lax.fori_loop(0, live_ref[0], one_slot, 0)

    for c in range(2):
        for b in range(own_blocks):
            at = slice(b * LANES, (b + 1) * LANES)
            out_ref[c, :, at] = grown[c, b, :tile_len, :]
            out_below_ref[c, :, at] = grown[c, b, tile_len:, :].astype(jnp.bfloat16)
        for b in range(side_blocks):
            at = slice(b * LANES, (b + 1) * LANES)
            out_right_ref[c, :, at] = grown[c, own_blocks + b, :tile_len, :].astype(jnp.bfloat16)
            out_corner_ref[c, :, at] = grown[c, own_blocks + b, tile_len:, :].astype(jnp.bfloat16)


def solve(live_total, shifts, own, right, below, corner, probe, measured, tables):
    tile_len = own.shape[1]
    side_len = probe.shape[1]
    blocks = (tile_len + side_len) // LANES
    smem = pl.BlockSpec(memory_space=pltpu.SMEM)
    vmem = pl.BlockSpec(memory_space=pltpu.VMEM)
    part = side_len // RADIX
    return pl.pallas_call(
        solve_kernel,
        out_shape=[
            jax.ShapeDtypeStruct(own.shape, jnp.float32),
            jax.ShapeDtypeStruct(right.shape, jnp.bfloat16),
            jax.ShapeDtypeStruct(below.shape, jnp.bfloat16),
            jax.ShapeDtypeStruct(corner.shape, jnp.bfloat16),
        ],
        in_specs=[smem, smem] + [vmem] * 8,
        out_specs=[vmem] * 4,
        scratch_shapes=[
            pltpu.VMEM((2, blocks, tile_len + side_len, LANES), jnp.float32),
            pltpu.VMEM((2, blocks, tile_len + side_len, LANES), jnp.float32),
            pltpu.VMEM((RADIX, 2 * part, side_len), jnp.bfloat16),
            pltpu.VMEM((RADIX, 2 * part, side_len), jnp.float32),
            pltpu.VMEM((RADIX, side_len, 2 * part), jnp.bfloat16),
        ],
        compiler_params=pltpu.CompilerParams(vmem_limit_bytes=60 * 1024 * 1024),
    )(live_total, shifts, own, right, below, corner, probe, measured, *tables)


def add_kernel(own_ref, left_ref, up_ref, out_ref):
    side_len = left_ref.shape[2]
    row_blocks = up_ref.shape[1] // own_ref.shape[1]
    total = own_ref[...]
    out_ref[:, :, :side_len] = total[:, :, :side_len] + left_ref[...].astype(jnp.float32)
    out_ref[:, :, side_len:] = total[:, :, side_len:]

    @pl.when(pl.program_id(0) < row_blocks)
    def _():
        height = own_ref.shape[1]
        at = pl.multiple_of(pl.program_id(0) * height, height)
        out_ref[...] += up_ref[:, pl.ds(at, height), :].astype(jnp.float32)


def add_received(own, from_left, from_up):
    height = LANES
    return pl.pallas_call(
        add_kernel,
        grid=(own.shape[1] // height,),
        out_shape=jax.ShapeDtypeStruct(own.shape, jnp.float32),
        in_specs=[
            pl.BlockSpec((2, height, own.shape[2]), lambda i: (0, i, 0)),
            pl.BlockSpec((2, height, from_left.shape[2]), lambda i: (0, i, 0)),
            pl.BlockSpec(memory_space=pltpu.VMEM),
        ],
        out_specs=pl.BlockSpec((2, height, own.shape[2]), lambda i: (0, i, 0)),
    )(own, from_left, from_up)


def shards(axes, object_slab, probe_field, intensities, offsets, live_count):
    right, below, corner, measured = gather(axes, object_slab, intensities[0, 0])
    live_total = live_count[lax.axis_index("scan")]
    tables = residue_tables(probe_field.shape[-1])
    own, spill, dropped, both = solve(
        live_total, offsets[0, 0], object_slab, right, below, corner, probe_field, measured, tables
    )
    from_left, from_up = scatter(axes, spill, dropped, both)
    return add_received(own, from_left, from_up)


def solution(mesh):
    placed = (
        P(None, "tile", "scan"),
        P(),
        P("scan", "tile", None, None, None),
        P("scan", "tile", None, None),
        P(None, "tile"),
    )
    axes = tuple((name, mesh.shape[name]) for name in ("scan", "tile"))
    return jax.shard_map(
        functools.partial(shards, axes), mesh=mesh, in_specs=placed, out_specs=P(None, "tile", "scan"), check_vma=False
    )
```

```python
import functools
import math

import jax
import jax.numpy as jnp
import numpy as np
from jax import lax
from jax.experimental import pallas as pl
from jax.experimental.pallas import tpu as pltpu
from jax.sharding import PartitionSpec as P

RADIX = 4
LANES = 128


def residue_tables(side_len):
    part = side_len // RADIX
    freq = np.arange(side_len).reshape(part, RADIX).T
    across = np.arange(part)
    phase = (freq[:, :, None] * across[None, None, :] % side_len) * (2.0 * math.pi / side_len)
    factor = 1.0 / math.sqrt(side_len)
    cos = np.cos(phase) * factor
    sin = np.sin(phase) * factor
    rows = np.concatenate(
        [np.concatenate([cos, sin], axis=2), np.concatenate([-sin, cos], axis=2)], axis=1
    ).astype(np.float32)
    return jnp.asarray(rows, jnp.bfloat16), jnp.asarray(rows.swapaxes(1, 2), jnp.bfloat16)


def sorted_by_residue(side_len):
    at = np.arange(side_len)
    source = at % (side_len // RADIX) * RADIX + at // (side_len // RADIX)
    sort = (source[:, None] == at[None, :]).astype(np.float32)
    return jnp.asarray(sort, jnp.bfloat16), jnp.asarray(sort.T, jnp.bfloat16)


def dot(a, b):
    return jnp.dot(a, b, preferred_element_type=jnp.float32)


def butterfly(parts, sign):
    (r0, i0), (r1, i1), (r2, i2), (r3, i3) = parts
    ar, ai, br, bi = r0 + r2, i0 + i2, r1 + r3, i1 + i3
    cr, ci, dr, di = r0 - r2, i0 - i2, r1 - r3, i1 - i3
    plus = (cr - di, ci + dr)
    minus = (cr + di, ci - dr)
    first, third = (plus, minus) if sign > 0 else (minus, plus)
    return [(ar + br, ai + bi), first, (ar - br, ai - bi), third]


def neighbours(axes):
    result = []
    for name, count in axes:
        me = lax.axis_index(name)
        result.append((me > 0, {name: me - 1}, me < count - 1, {name: me + 1}))
    return result


def meet(peers):
    barrier = pltpu.get_barrier_semaphore()
    for has_low, low, has_high, high in peers:
        for there, peer in ((has_low, low), (has_high, high)):

            @pl.when(there)
            def _(peer=peer):
                pl.semaphore_signal(
                    barrier, inc=1, device_id=peer, device_id_type=pl.DeviceIdType.MESH
                )

    count = sum(
        there.astype(jnp.int32) for has_low, _, has_high, _ in peers for there in (has_low, has_high)
    )
    pl.semaphore_wait(barrier, count)


def remote(source, target, sends, receives, index, peer):
    return pltpu.make_async_remote_copy(
        src_ref=source,
        dst_ref=target,
        send_sem=sends.at[index],
        recv_sem=receives.at[index],
        device_id=peer,
        device_id_type=pl.DeviceIdType.MESH,
    )


def gather_kernel(
    axes,
    own_hbm,
    measured_hbm,
    sort_hbm,
    unsort_hbm,
    right_hbm,
    below_hbm,
    corner_hbm,
    sorted_hbm,
    own,
    sent,
    right,
    below,
    corner,
    measured,
    arranged,
    sort,
    unsort,
    sends,
    receives,
    fetches,
    puts,
):
    side_len = measured.shape[-1]
    scan, tile = neighbours(axes)
    has_left, left, has_right, _ = scan
    has_up, up, has_down, _ = tile
    first = pltpu.make_async_copy(
        own_hbm.at[:, :side_len, :side_len], own.at[:, :side_len, :side_len], fetches.at[0]
    )
    second = pltpu.make_async_copy(
        own_hbm.at[:, side_len:, :side_len], own.at[:, side_len:, :side_len], fetches.at[1]
    )
    third = pltpu.make_async_copy(
        own_hbm.at[:, :side_len, side_len:], own.at[:, :side_len, side_len:], fetches.at[2]
    )
    fetch_measured = pltpu.make_async_copy(measured_hbm, measured, fetches.at[3])
    fetch_sort = pltpu.make_async_copy(sort_hbm, sort, fetches.at[4])
    fetch_unsort = pltpu.make_async_copy(unsort_hbm, unsort, fetches.at[5])
    first.start()
    second.start()
    third.start()
    fetch_sort.start()
    fetch_unsort.start()
    fetch_measured.start()
    top = remote(
        sent.at[:, :side_len, :side_len], right.at[:, :side_len, :], sends, receives, 0, left
    )
    rest = remote(
        sent.at[:, side_len:, :side_len], right.at[:, side_len:, :], sends, receives, 1, left
    )
    under = remote(sent.at[:, :side_len, :], below, sends, receives, 2, up)
    across = remote(right.at[:, :side_len, :], corner, sends, receives, 3, up)
    first.wait()
    sent[:, :side_len, :side_len] = own[:, :side_len, :side_len].astype(jnp.bfloat16)
    meet((scan, tile))

    @pl.when(has_left)
    def _():
        top.start()

    second.wait()
    third.wait()
    sent[:, side_len:, :side_len] = own[:, side_len:, :side_len].astype(jnp.bfloat16)
    sent[:, :side_len, side_len:] = own[:, :side_len, side_len:].astype(jnp.bfloat16)

    @pl.when(has_left)
    def _():
        rest.start()

    @pl.when(has_up)
    def _():
        under.start()

    @pl.when(jnp.logical_not(has_right))
    def _():
        right[...] = jnp.zeros_like(right)

    @pl.when(jnp.logical_not(has_down))
    def _():
        below[...] = jnp.zeros_like(below)
        corner[...] = jnp.zeros_like(corner)

    fetch_sort.wait()
    fetch_unsort.wait()
    fetch_measured.wait()

    def sort_slot(slot, carry):
        rows = dot(sort[...], measured[slot]).astype(jnp.bfloat16)
        arranged[slot] = dot(rows, unsort[...]).astype(jnp.bfloat16)
        return carry

    lax.fori_loop(0, measured.shape[0], sort_slot, 0)
    put_sorted = pltpu.make_async_copy(arranged, sorted_hbm, puts.at[0])
    put_sorted.start()

    @pl.when(has_right)
    def _():
        top.wait_recv()

    @pl.when(has_up)
    def _():
        across.start()

    put_top = pltpu.make_async_copy(
        right.at[:, :side_len, :], right_hbm.at[:, :side_len, :], puts.at[1]
    )
    put_top.start()

    @pl.when(has_down)
    def _():
        under.wait_recv()

    put_below = pltpu.make_async_copy(below, below_hbm, puts.at[2])
    put_below.start()

    @pl.when(has_right)
    def _():
        rest.wait_recv()

    put_rest = pltpu.make_async_copy(
        right.at[:, side_len:, :], right_hbm.at[:, side_len:, :], puts.at[3]
    )
    put_rest.start()

    @pl.when(has_down)
    def _():
        across.wait_recv()

    put_corner = pltpu.make_async_copy(corner, corner_hbm, puts.at[4])
    put_corner.start()

    @pl.when(has_left)
    def _():
        top.wait_send()
        rest.wait_send()

    @pl.when(has_up)
    def _():
        under.wait_send()
        across.wait_send()

    put_sorted.wait()
    put_top.wait()
    put_below.wait()
    put_rest.wait()
    put_corner.wait()


def gather(axes, own, measured):
    side_len = measured.shape[-1]
    tile_len = own.shape[1]
    hbm = pl.BlockSpec(memory_space=pltpu.HBM)
    right = (2, tile_len, side_len)
    below = (2, side_len, tile_len)
    corner = (2, side_len, side_len)
    return pl.pallas_call(
        functools.partial(gather_kernel, axes),
        out_shape=[
            jax.ShapeDtypeStruct(shape, jnp.bfloat16)
            for shape in (right, below, corner, measured.shape)
        ],
        in_specs=[hbm] * 4,
        out_specs=[hbm] * 4,
        scratch_shapes=[
            pltpu.VMEM(own.shape, jnp.float32),
            pltpu.VMEM(own.shape, jnp.bfloat16),
            pltpu.VMEM(right, jnp.bfloat16),
            pltpu.VMEM(below, jnp.bfloat16),
            pltpu.VMEM(corner, jnp.bfloat16),
            pltpu.VMEM(measured.shape, jnp.bfloat16),
            pltpu.VMEM(measured.shape, jnp.bfloat16),
            pltpu.VMEM((side_len, side_len), jnp.bfloat16),
            pltpu.VMEM((side_len, side_len), jnp.bfloat16),
            pltpu.SemaphoreType.DMA((4,)),
            pltpu.SemaphoreType.DMA((4,)),
            pltpu.SemaphoreType.DMA((6,)),
            pltpu.SemaphoreType.DMA((5,)),
        ],
        compiler_params=pltpu.CompilerParams(
            collective_id=0, has_side_effects=True, vmem_limit_bytes=48 * 1024 * 1024
        ),
    )(own, measured, *sorted_by_residue(side_len))


def scatter_kernel(
    axes,
    own_hbm,
    spill_hbm,
    drop_hbm,
    both_hbm,
    out_hbm,
    total,
    spill,
    joined,
    landed,
    from_left,
    from_up,
    sends,
    receives,
    fetches,
    puts,
):
    side_len = landed.shape[1]
    scan, tile = neighbours(axes)
    has_left, _, has_right, right = scan
    has_up, _, has_down, down = tile
    fetch_spill = pltpu.make_async_copy(spill_hbm.at[:, :side_len, :], spill, fetches.at[0])
    fetch_own = pltpu.make_async_copy(own_hbm, total, fetches.at[1])
    fetch_spill.start()
    fetch_own.start()
    meet((scan, tile))
    corner = remote(both_hbm, landed, sends, receives, 0, down)
    under = remote(drop_hbm, from_up, sends, receives, 1, down)
    rest = remote(
        spill_hbm.at[:, side_len:, :], from_left.at[:, side_len:, :], sends, receives, 2, right
    )
    top = remote(joined, from_left.at[:, :side_len, :], sends, receives, 3, right)

    @pl.when(has_down)
    def _():
        corner.start()

    @pl.when(has_right)
    def _():
        rest.start()

    @pl.when(has_down)
    def _():
        under.start()

    @pl.when(jnp.logical_not(has_up))
    def _():
        landed[...] = jnp.zeros_like(landed)

    fetch_spill.wait()

    @pl.when(has_up)
    def _():
        corner.wait_recv()

    joined[...] = (spill[...].astype(jnp.float32) + landed[...].astype(jnp.float32)).astype(
        jnp.bfloat16
    )

    @pl.when(has_right)
    def _():
        top.start()

    fetch_own.wait()

    @pl.when(has_left)
    def _():
        rest.wait_recv()
        total[:, side_len:, :side_len] += from_left[:, side_len:, :].astype(jnp.float32)

    put_rest = pltpu.make_async_copy(
        total.at[:, side_len:, :], out_hbm.at[:, side_len:, :], puts.at[0]
    )
    put_rest.start()

    @pl.when(has_up)
    def _():
        under.wait_recv()
        total[:, :side_len, :] += from_up[...].astype(jnp.float32)

    put_far = pltpu.make_async_copy(
        total.at[:, :side_len, side_len:], out_hbm.at[:, :side_len, side_len:], puts.at[1]
    )
    put_far.start()

    @pl.when(has_left)
    def _():
        top.wait_recv()
        total[:, :side_len, :side_len] += from_left[:, :side_len, :].astype(jnp.float32)

    put_top = pltpu.make_async_copy(
        total.at[:, :side_len, :side_len], out_hbm.at[:, :side_len, :side_len], puts.at[2]
    )
    put_top.start()

    @pl.when(has_right)
    def _():
        rest.wait_send()
        top.wait_send()

    @pl.when(has_down)
    def _():
        corner.wait_send()
        under.wait_send()

    put_rest.wait()
    put_far.wait()
    put_top.wait()


def scatter(axes, own, spill, dropped, both):
    hbm = pl.BlockSpec(memory_space=pltpu.HBM)
    return pl.pallas_call(
        functools.partial(scatter_kernel, axes),
        out_shape=jax.ShapeDtypeStruct(own.shape, jnp.float32),
        in_specs=[hbm] * 4,
        out_specs=hbm,
        scratch_shapes=[
            pltpu.VMEM(own.shape, jnp.float32),
            pltpu.VMEM(both.shape, jnp.bfloat16),
            pltpu.VMEM(both.shape, jnp.bfloat16),
            pltpu.VMEM(both.shape, jnp.bfloat16),
            pltpu.VMEM(spill.shape, jnp.bfloat16),
            pltpu.VMEM(dropped.shape, jnp.bfloat16),
            pltpu.SemaphoreType.DMA((4,)),
            pltpu.SemaphoreType.DMA((4,)),
            pltpu.SemaphoreType.DMA((2,)),
            pltpu.SemaphoreType.DMA((3,)),
        ],
        compiler_params=pltpu.CompilerParams(
            collective_id=1, has_side_effects=True, vmem_limit_bytes=40 * 1024 * 1024
        ),
    )(own, spill, dropped, both)


def solve_kernel(
    live_ref,
    shift_ref,
    own_hbm,
    right_hbm,
    below_hbm,
    corner_hbm,
    probe_hbm,
    measured_hbm,
    rows_hbm,
    cols_hbm,
    out_hbm,
    out_right_hbm,
    out_below_hbm,
    out_corner_hbm,
    field,
    grown,
    mixed,
    spectra,
    backs,
    right_ref,
    below_ref,
    corner_ref,
    probe_ref,
    measured_ref,
    rows_ref,
    cols_ref,
    fetches,
    puts,
):
    tile_len = own_hbm.shape[1]
    side_len = probe_ref.shape[1]
    part = side_len // RADIX
    own_blocks = tile_len // LANES
    side_blocks = side_len // LANES
    lane = lax.broadcasted_iota(jnp.int32, (1, LANES), 1)

    loads = [
        pltpu.make_async_copy(source, target, fetches.at[i])
        for i, (source, target) in enumerate(
            (
                (below_hbm, below_ref),
                (right_hbm, right_ref),
                (corner_hbm, corner_ref),
                (probe_hbm, probe_ref),
                (rows_hbm, rows_ref),
                (cols_hbm, cols_ref),
                (measured_hbm, measured_ref),
            )
        )
    ]
    for load in loads[:3]:
        load.start()
    pieces = [
        pltpu.make_async_copy(
            own_hbm.at[c, :, b * LANES : (b + 1) * LANES],
            field.at[c, b, :tile_len, :],
            fetches.at[len(loads) + c * own_blocks + b],
        )
        for c in range(2)
        for b in range(own_blocks)
    ]
    for load in pieces + loads[3:]:
        load.start()
    grown[...] = jnp.zeros_like(grown)
    loads[0].wait()
    for c in range(2):
        for b in range(own_blocks):
            at = slice(b * LANES, (b + 1) * LANES)
            field[c, b, tile_len:, :] = below_ref[c, :, at].astype(jnp.float32)
    loads[1].wait()
    loads[2].wait()
    for c in range(2):
        for b in range(side_blocks):
            at = slice(b * LANES, (b + 1) * LANES)
            field[c, own_blocks + b, :tile_len, :] = right_ref[c, :, at].astype(jnp.float32)
            field[c, own_blocks + b, tile_len:, :] = corner_ref[c, :, at].astype(jnp.float32)
    for load in pieces + loads[3:]:
        load.wait()

    def one_slot(slot, carry):
        row = shift_ref[slot, 0]
        col = shift_ref[slot, 1]
        block = lax.div(col, LANES)
        turn = lax.rem(col, LANES)
        back_turn = lax.rem(LANES - turn, LANES)
        keep = lane < LANES - turn
        enter = lane >= turn
        height = 16

        def load_rows(i, carry):
            at = pl.multiple_of(i * height, height)
            waves = []
            for p in range(RADIX):
                cuts = []
                for c in range(2):
                    turned = [
                        pltpu.roll(
                            field[c, block + b, pl.ds(row + at + p * part, height), :], back_turn, 1
                        )
                        for b in range(side_blocks + 1)
                    ]
                    cuts.append(
                        [jnp.where(keep, turned[b], turned[b + 1]) for b in range(side_blocks)]
                    )
                blocks = []
                for b in range(side_blocks):
                    cols = slice(b * LANES, (b + 1) * LANES)
                    probe_re = probe_ref[0, pl.ds(at + p * part, height), cols]
                    probe_im = probe_ref[1, pl.ds(at + p * part, height), cols]
                    re, im = cuts[0][b], cuts[1][b]
                    blocks.append((probe_re * re - probe_im * im, probe_re * im + probe_im * re))
                waves.append(blocks)
            for b in range(side_blocks):
                cols = slice(b * LANES, (b + 1) * LANES)
                sums = butterfly([waves[p][b] for p in range(RADIX)], -1)
                for q in range(RADIX):
                    mixed[q, pl.ds(at, height), cols] = sums[q][0].astype(jnp.bfloat16)
                    mixed[q, pl.ds(at + part, height), cols] = sums[q][1].astype(jnp.bfloat16)
            return carry

        lax.fori_loop(0, part // height, load_rows, 0, unroll=part // height)

        for q in range(RADIX):
            half = dot(rows_ref[q], mixed[q])
            parts = [
                (half[:part, p * part : (p + 1) * part], half[part:, p * part : (p + 1) * part])
                for p in range(RADIX)
            ]
            misfits = []
            for other, (re, im) in enumerate(butterfly(parts, -1)):
                far = dot(jnp.concatenate([re, im], axis=1).astype(jnp.bfloat16), cols_ref[other])
                far_re, far_im = far[:, :part], far[:, part:]
                seen = measured_ref[
                    slot, q * part : (q + 1) * part, other * part : (other + 1) * part
                ].astype(jnp.float32)
                misfit = far_re * far_re + far_im * far_im - seen
                misfits.append(
                    jnp.concatenate([misfit * far_re, misfit * far_im], axis=0).astype(jnp.bfloat16)
                )
            spectra[q] = dot(cols_ref[q], jnp.concatenate(misfits, axis=1))

        def mix_rows(i, carry):
            at = pl.multiple_of(i * height, height)
            for other in range(RADIX):
                cols = slice(other * part, (other + 1) * part)
                parts = [
                    (spectra[q, pl.ds(at, height), cols], spectra[q, pl.ds(at + part, height), cols])
                    for q in range(RADIX)
                ]
                for p, (re, im) in enumerate(butterfly(parts, 1)):
                    backs[other, pl.ds(at + p * part, height), :] = jnp.concatenate(
                        [re, im], axis=1
                    ).astype(jnp.bfloat16)
            return carry

        lax.fori_loop(0, part // height, mix_rows, 0, unroll=part // height)

        def add_rows(i, carry):
            tall = 256
            at = pl.multiple_of(i * tall, tall)
            parts = []
            for other in range(RADIX):
                grad = dot(backs[other, pl.ds(at, tall), :], rows_ref[other])
                parts.append((grad[:, :part], grad[:, part:]))
            turned = [[], []]
            for b, (re, im) in enumerate(butterfly(parts, 1)):
                cols = slice(b * part, (b + 1) * part)
                probe_re = probe_ref[0, pl.ds(at, tall), cols]
                probe_im = probe_ref[1, pl.ds(at, tall), cols]
                turned[0].append(pltpu.roll(probe_re * re + probe_im * im, turn, 1))
                turned[1].append(pltpu.roll(probe_re * im - probe_im * re, turn, 1))
            for c in range(2):
                for b in range(side_blocks + 1):
                    if b == 0:
                        value = jnp.where(enter, turned[c][0], 0.0)
                    elif b == side_blocks:
                        value = jnp.where(enter, 0.0, turned[c][b - 1])
                    else:
                        value = jnp.where(enter, turned[c][b], turned[c][b - 1])
                    grown[c, block + b, pl.ds(row + at, tall), :] += value
            return carry

        lax.fori_loop(0, side_len // 256, add_rows, 0)
        return carry

    lax.fori_loop(0, live_ref[0], one_slot, 0)

    stores = [
        pltpu.make_async_copy(
            grown.at[c, b, :tile_len, :],
            out_hbm.at[c, :, b * LANES : (b + 1) * LANES],
            puts.at[3 + c * own_blocks + b],
        )
        for c in range(2)
        for b in range(own_blocks)
    ]
    for store in stores:
        store.start()
    for c in range(2):
        for b in range(side_blocks):
            at = slice(b * LANES, (b + 1) * LANES)
            corner_ref[c, :, at] = grown[c, own_blocks + b, tile_len:, :].astype(jnp.bfloat16)
            right_ref[c, :, at] = grown[c, own_blocks + b, :tile_len, :].astype(jnp.bfloat16)
    stores.append(pltpu.make_async_copy(corner_ref, out_corner_hbm, puts.at[0]))
    stores.append(pltpu.make_async_copy(right_ref, out_right_hbm, puts.at[1]))
    stores[-2].start()
    stores[-1].start()
    for c in range(2):
        for b in range(own_blocks):
            at = slice(b * LANES, (b + 1) * LANES)
            below_ref[c, :, at] = grown[c, b, tile_len:, :].astype(jnp.bfloat16)
    stores.append(pltpu.make_async_copy(below_ref, out_below_hbm, puts.at[2]))
    stores[-1].start()
    for store in stores:
        store.wait()


def solve(live_total, shifts, own, right, below, corner, probe, measured, tables):
    tile_len = own.shape[1]
    side_len = probe.shape[1]
    blocks = (tile_len + side_len) // LANES
    smem = pl.BlockSpec(memory_space=pltpu.SMEM)
    hbm = pl.BlockSpec(memory_space=pltpu.HBM)
    part = side_len // RADIX
    copies = 2 * (tile_len // LANES)
    return pl.pallas_call(
        solve_kernel,
        out_shape=[
            jax.ShapeDtypeStruct(own.shape, jnp.float32),
            jax.ShapeDtypeStruct(right.shape, jnp.bfloat16),
            jax.ShapeDtypeStruct(below.shape, jnp.bfloat16),
            jax.ShapeDtypeStruct(corner.shape, jnp.bfloat16),
        ],
        in_specs=[smem, smem] + [hbm] * 8,
        out_specs=[hbm] * 4,
        scratch_shapes=[
            pltpu.VMEM((2, blocks, tile_len + side_len, LANES), jnp.float32),
            pltpu.VMEM((2, blocks, tile_len + side_len, LANES), jnp.float32),
            pltpu.VMEM((RADIX, 2 * part, side_len), jnp.bfloat16),
            pltpu.VMEM((RADIX, 2 * part, side_len), jnp.float32),
            pltpu.VMEM((RADIX, side_len, 2 * part), jnp.bfloat16),
            pltpu.VMEM(right.shape, jnp.bfloat16),
            pltpu.VMEM(below.shape, jnp.bfloat16),
            pltpu.VMEM(corner.shape, jnp.bfloat16),
            pltpu.VMEM(probe.shape, jnp.float32),
            pltpu.VMEM(measured.shape, jnp.bfloat16),
            pltpu.VMEM(tables[0].shape, jnp.bfloat16),
            pltpu.VMEM(tables[1].shape, jnp.bfloat16),
            pltpu.SemaphoreType.DMA((7 + copies,)),
            pltpu.SemaphoreType.DMA((3 + copies,)),
        ],
        compiler_params=pltpu.CompilerParams(vmem_limit_bytes=60 * 1024 * 1024),
    )(live_total, shifts, own, right, below, corner, probe, measured, *tables)


def shards(axes, object_slab, probe_field, intensities, offsets, live_count):
    right, below, corner, measured = gather(axes, object_slab, intensities[0, 0])
    live_total = live_count[lax.axis_index("scan")]
    tables = residue_tables(probe_field.shape[-1])
    own, spill, dropped, both = solve(
        live_total, offsets[0, 0], object_slab, right, below, corner, probe_field, measured, tables
    )
    return scatter(axes, own, spill, dropped, both)


def solution(mesh):
    placed = (
        P(None, "tile", "scan"),
        P(),
        P("scan", "tile", None, None, None),
        P("scan", "tile", None, None),
        P(None, "tile"),
    )
    axes = tuple((name, mesh.shape[name]) for name in ("scan", "tile"))
    return jax.shard_map(
        functools.partial(shards, axes), mesh=mesh, in_specs=placed, out_specs=P(None, "tile", "scan"), check_vma=False
    )
```

```python
import functools
import math

import jax
import jax.numpy as jnp
import numpy as np
from jax import lax
from jax.experimental import pallas as pl
from jax.experimental.pallas import tpu as pltpu
from jax.sharding import PartitionSpec as P

RADIX = 4
LANES = 128
vmem_bytes = 67043328


def residue_tables(side_len):
    part = side_len // RADIX
    freq = np.arange(side_len).reshape(part, RADIX).T
    across = np.arange(part)
    phase = (freq[:, :, None] * across[None, None, :] % side_len) * (2.0 * math.pi / side_len)
    factor = 1.0 / math.sqrt(side_len)
    cos = np.cos(phase) * factor
    sin = np.sin(phase) * factor
    rows = np.concatenate(
        [np.concatenate([cos, sin], axis=2), np.concatenate([-sin, cos], axis=2)], axis=1
    ).astype(np.float32)
    return jnp.asarray(rows, jnp.bfloat16), jnp.asarray(rows.swapaxes(1, 2), jnp.bfloat16)


def sorted_by_residue(side_len):
    at = np.arange(side_len)
    source = at % (side_len // RADIX) * RADIX + at // (side_len // RADIX)
    sort = (source[:, None] == at[None, :]).astype(np.float32)
    return jnp.asarray(sort, jnp.bfloat16), jnp.asarray(sort.T, jnp.bfloat16)


def dot(a, b):
    return jnp.dot(a, b, preferred_element_type=jnp.float32)


def butterfly(parts, sign):
    (r0, i0), (r1, i1), (r2, i2), (r3, i3) = parts
    ar, ai, br, bi = r0 + r2, i0 + i2, r1 + r3, i1 + i3
    cr, ci, dr, di = r0 - r2, i0 - i2, r1 - r3, i1 - i3
    plus = (cr - di, ci + dr)
    minus = (cr + di, ci - dr)
    first, third = (plus, minus) if sign > 0 else (minus, plus)
    return [(ar + br, ai + bi), first, (ar - br, ai - bi), third]


def neighbours(axes):
    result = []
    for name, count in axes:
        me = lax.axis_index(name)
        result.append((me > 0, {name: me - 1}, me < count - 1, {name: me + 1}))
    return result


def meet(peers):
    barrier = pltpu.get_barrier_semaphore()
    for has_low, low, has_high, high in peers:
        for there, peer in ((has_low, low), (has_high, high)):

            @pl.when(there)
            def _(peer=peer):
                pl.semaphore_signal(
                    barrier, inc=1, device_id=peer, device_id_type=pl.DeviceIdType.MESH
                )

    count = sum(
        there.astype(jnp.int32) for has_low, _, has_high, _ in peers for there in (has_low, has_high)
    )
    pl.semaphore_wait(barrier, count)


def remote(source, target, sends, receives, index, peer):
    return pltpu.make_async_remote_copy(
        src_ref=source,
        dst_ref=target,
        send_sem=sends.at[index],
        recv_sem=receives.at[index],
        device_id=peer,
        device_id_type=pl.DeviceIdType.MESH,
    )


def gather_kernel(
    axes,
    own_hbm,
    measured_hbm,
    sort_hbm,
    unsort_hbm,
    right_hbm,
    below_hbm,
    corner_hbm,
    sorted_hbm,
    own,
    sent,
    right,
    below,
    corner,
    measured,
    arranged,
    sort,
    unsort,
    sends,
    receives,
    fetches,
    puts,
):
    side_len = measured.shape[-1]
    scan, tile = neighbours(axes)
    has_left, left, has_right, _ = scan
    has_up, up, has_down, _ = tile
    first = pltpu.make_async_copy(
        own_hbm.at[:, :side_len, :side_len], own.at[:, :side_len, :side_len], fetches.at[0]
    )
    second = pltpu.make_async_copy(
        own_hbm.at[:, side_len:, :side_len], own.at[:, side_len:, :side_len], fetches.at[1]
    )
    third = pltpu.make_async_copy(
        own_hbm.at[:, :side_len, side_len:], own.at[:, :side_len, side_len:], fetches.at[2]
    )
    fetch_measured = pltpu.make_async_copy(measured_hbm, measured, fetches.at[3])
    fetch_sort = pltpu.make_async_copy(sort_hbm, sort, fetches.at[4])
    fetch_unsort = pltpu.make_async_copy(unsort_hbm, unsort, fetches.at[5])
    first.start()
    second.start()
    third.start()
    fetch_sort.start()
    fetch_unsort.start()
    fetch_measured.start()
    top = remote(
        sent.at[:, :side_len, :side_len], right.at[:, :side_len, :], sends, receives, 0, left
    )
    rest = remote(
        sent.at[:, side_len:, :side_len], right.at[:, side_len:, :], sends, receives, 1, left
    )
    under = remote(sent.at[:, :side_len, :], below, sends, receives, 2, up)
    across = remote(right.at[:, :side_len, :], corner, sends, receives, 3, up)
    first.wait()
    sent[:, :side_len, :side_len] = own[:, :side_len, :side_len].astype(jnp.bfloat16)
    meet((scan, tile))

    @pl.when(has_left)
    def _():
        top.start()

    second.wait()
    third.wait()
    sent[:, side_len:, :side_len] = own[:, side_len:, :side_len].astype(jnp.bfloat16)
    sent[:, :side_len, side_len:] = own[:, :side_len, side_len:].astype(jnp.bfloat16)

    @pl.when(has_left)
    def _():
        rest.start()

    @pl.when(has_up)
    def _():
        under.start()

    @pl.when(jnp.logical_not(has_right))
    def _():
        right[...] = jnp.zeros_like(right)

    @pl.when(jnp.logical_not(has_down))
    def _():
        below[...] = jnp.zeros_like(below)
        corner[...] = jnp.zeros_like(corner)

    fetch_sort.wait()
    fetch_unsort.wait()
    fetch_measured.wait()

    def sort_slot(slot, carry):
        rows = dot(sort[...], measured[slot]).astype(jnp.bfloat16)
        arranged[slot] = dot(rows, unsort[...]).astype(jnp.bfloat16)
        return carry

    lax.fori_loop(0, measured.shape[0], sort_slot, 0)
    put_sorted = pltpu.make_async_copy(arranged, sorted_hbm, puts.at[0])
    put_sorted.start()

    @pl.when(has_right)
    def _():
        top.wait_recv()

    @pl.when(has_up)
    def _():
        across.start()

    put_top = pltpu.make_async_copy(
        right.at[:, :side_len, :], right_hbm.at[:, :side_len, :], puts.at[1]
    )
    put_top.start()

    @pl.when(has_down)
    def _():
        under.wait_recv()

    put_below = pltpu.make_async_copy(below, below_hbm, puts.at[2])
    put_below.start()

    @pl.when(has_right)
    def _():
        rest.wait_recv()

    put_rest = pltpu.make_async_copy(
        right.at[:, side_len:, :], right_hbm.at[:, side_len:, :], puts.at[3]
    )
    put_rest.start()

    @pl.when(has_down)
    def _():
        across.wait_recv()

    put_corner = pltpu.make_async_copy(corner, corner_hbm, puts.at[4])
    put_corner.start()

    @pl.when(has_left)
    def _():
        top.wait_send()
        rest.wait_send()

    @pl.when(has_up)
    def _():
        under.wait_send()
        across.wait_send()

    put_sorted.wait()
    put_top.wait()
    put_below.wait()
    put_rest.wait()
    put_corner.wait()


def gather(axes, own, measured):
    side_len = measured.shape[-1]
    tile_len = own.shape[1]
    hbm = pl.BlockSpec(memory_space=pltpu.HBM)
    right = (2, tile_len, side_len)
    below = (2, side_len, tile_len)
    corner = (2, side_len, side_len)
    return pl.pallas_call(
        functools.partial(gather_kernel, axes),
        out_shape=[
            jax.ShapeDtypeStruct(shape, jnp.bfloat16)
            for shape in (right, below, corner, measured.shape)
        ],
        in_specs=[hbm] * 4,
        out_specs=[hbm] * 4,
        scratch_shapes=[
            pltpu.VMEM(own.shape, jnp.float32),
            pltpu.VMEM(own.shape, jnp.bfloat16),
            pltpu.VMEM(right, jnp.bfloat16),
            pltpu.VMEM(below, jnp.bfloat16),
            pltpu.VMEM(corner, jnp.bfloat16),
            pltpu.VMEM(measured.shape, jnp.bfloat16),
            pltpu.VMEM(measured.shape, jnp.bfloat16),
            pltpu.VMEM((side_len, side_len), jnp.bfloat16),
            pltpu.VMEM((side_len, side_len), jnp.bfloat16),
            pltpu.SemaphoreType.DMA((4,)),
            pltpu.SemaphoreType.DMA((4,)),
            pltpu.SemaphoreType.DMA((6,)),
            pltpu.SemaphoreType.DMA((5,)),
        ],
        compiler_params=pltpu.CompilerParams(
            collective_id=0, has_side_effects=True, vmem_limit_bytes=vmem_bytes
        ),
    )(own, measured, *sorted_by_residue(side_len))


def scatter_kernel(
    axes,
    own_hbm,
    spill_hbm,
    drop_hbm,
    both_hbm,
    out_hbm,
    total,
    spill,
    joined,
    landed,
    from_left,
    from_up,
    sends,
    receives,
    fetches,
    puts,
):
    side_len = landed.shape[1]
    scan, tile = neighbours(axes)
    has_left, _, has_right, right = scan
    has_up, _, has_down, down = tile
    fetch_spill = pltpu.make_async_copy(spill_hbm.at[:, :side_len, :], spill, fetches.at[0])
    fetch_own = pltpu.make_async_copy(own_hbm, total, fetches.at[1])
    fetch_spill.start()
    fetch_own.start()
    meet((scan, tile))
    corner = remote(both_hbm, landed, sends, receives, 0, down)
    under = remote(drop_hbm, from_up, sends, receives, 1, down)
    rest = remote(
        spill_hbm.at[:, side_len:, :], from_left.at[:, side_len:, :], sends, receives, 2, right
    )
    top = remote(joined, from_left.at[:, :side_len, :], sends, receives, 3, right)

    @pl.when(has_down)
    def _():
        corner.start()

    @pl.when(has_right)
    def _():
        rest.start()

    @pl.when(has_down)
    def _():
        under.start()

    @pl.when(jnp.logical_not(has_up))
    def _():
        landed[...] = jnp.zeros_like(landed)

    fetch_spill.wait()

    @pl.when(has_up)
    def _():
        corner.wait_recv()

    joined[...] = (spill[...].astype(jnp.float32) + landed[...].astype(jnp.float32)).astype(
        jnp.bfloat16
    )

    @pl.when(has_right)
    def _():
        top.start()

    fetch_own.wait()

    @pl.when(has_left)
    def _():
        rest.wait_recv()
        total[:, side_len:, :side_len] += from_left[:, side_len:, :].astype(jnp.float32)

    put_rest = pltpu.make_async_copy(
        total.at[:, side_len:, :], out_hbm.at[:, side_len:, :], puts.at[0]
    )
    put_rest.start()

    @pl.when(has_up)
    def _():
        under.wait_recv()
        total[:, :side_len, :] += from_up[...].astype(jnp.float32)

    put_far = pltpu.make_async_copy(
        total.at[:, :side_len, side_len:], out_hbm.at[:, :side_len, side_len:], puts.at[1]
    )
    put_far.start()

    @pl.when(has_left)
    def _():
        top.wait_recv()
        total[:, :side_len, :side_len] += from_left[:, :side_len, :].astype(jnp.float32)

    put_top = pltpu.make_async_copy(
        total.at[:, :side_len, :side_len], out_hbm.at[:, :side_len, :side_len], puts.at[2]
    )
    put_top.start()

    @pl.when(has_right)
    def _():
        rest.wait_send()
        top.wait_send()

    @pl.when(has_down)
    def _():
        corner.wait_send()
        under.wait_send()

    put_rest.wait()
    put_far.wait()
    put_top.wait()


def scatter(axes, own, spill, dropped, both):
    hbm = pl.BlockSpec(memory_space=pltpu.HBM)
    return pl.pallas_call(
        functools.partial(scatter_kernel, axes),
        out_shape=jax.ShapeDtypeStruct(own.shape, jnp.float32),
        in_specs=[hbm] * 4,
        out_specs=hbm,
        scratch_shapes=[
            pltpu.VMEM(own.shape, jnp.float32),
            pltpu.VMEM(both.shape, jnp.bfloat16),
            pltpu.VMEM(both.shape, jnp.bfloat16),
            pltpu.VMEM(both.shape, jnp.bfloat16),
            pltpu.VMEM(spill.shape, jnp.bfloat16),
            pltpu.VMEM(dropped.shape, jnp.bfloat16),
            pltpu.SemaphoreType.DMA((4,)),
            pltpu.SemaphoreType.DMA((4,)),
            pltpu.SemaphoreType.DMA((2,)),
            pltpu.SemaphoreType.DMA((3,)),
        ],
        compiler_params=pltpu.CompilerParams(
            collective_id=1, has_side_effects=True, vmem_limit_bytes=vmem_bytes
        ),
    )(own, spill, dropped, both)


def solve_kernel(
    live_ref,
    shift_ref,
    own_hbm,
    right_hbm,
    below_hbm,
    corner_hbm,
    probe_hbm,
    measured_hbm,
    rows_hbm,
    cols_hbm,
    out_hbm,
    out_right_hbm,
    out_below_hbm,
    out_corner_hbm,
    field,
    grown,
    mixed,
    spectra,
    backs,
    right_ref,
    below_ref,
    corner_ref,
    probe_ref,
    measured_ref,
    rows_ref,
    cols_ref,
    fetches,
    puts,
):
    tile_len = own_hbm.shape[1]
    side_len = probe_ref.shape[1]
    part = side_len // RADIX
    own_blocks = tile_len // LANES
    side_blocks = side_len // LANES
    lane = lax.broadcasted_iota(jnp.int32, (1, LANES), 1)

    loads = [
        pltpu.make_async_copy(source, target, fetches.at[i])
        for i, (source, target) in enumerate(
            (
                (below_hbm, below_ref),
                (right_hbm, right_ref),
                (corner_hbm, corner_ref),
                (probe_hbm, probe_ref),
                (rows_hbm, rows_ref),
                (cols_hbm, cols_ref),
                (measured_hbm, measured_ref),
            )
        )
    ]
    for load in loads[:3]:
        load.start()
    pieces = [
        pltpu.make_async_copy(
            own_hbm.at[c, :, b * LANES : (b + 1) * LANES],
            field.at[c, b, :tile_len, :],
            fetches.at[len(loads) + c * own_blocks + b],
        )
        for c in range(2)
        for b in range(own_blocks)
    ]
    for load in pieces + loads[3:]:
        load.start()
    grown[...] = jnp.zeros_like(grown)
    loads[0].wait()
    for c in range(2):
        for b in range(own_blocks):
            at = slice(b * LANES, (b + 1) * LANES)
            field[c, b, tile_len:, :] = below_ref[c, :, at].astype(jnp.float32)
    loads[1].wait()
    loads[2].wait()
    for c in range(2):
        for b in range(side_blocks):
            at = slice(b * LANES, (b + 1) * LANES)
            field[c, own_blocks + b, :tile_len, :] = right_ref[c, :, at].astype(jnp.float32)
            field[c, own_blocks + b, tile_len:, :] = corner_ref[c, :, at].astype(jnp.float32)
    for load in pieces + loads[3:]:
        load.wait()

    def one_slot(slot, carry):
        row = shift_ref[0, slot]
        col = shift_ref[1, slot]
        block = lax.div(col, LANES)
        turn = lax.rem(col, LANES)
        back_turn = lax.rem(LANES - turn, LANES)
        keep = lane < LANES - turn
        enter = lane >= turn
        height = 16

        def load_rows(i, carry):
            at = pl.multiple_of(i * height, height)
            waves = []
            for p in range(RADIX):
                cuts = []
                for c in range(2):
                    turned = [
                        pltpu.roll(
                            field[c, block + b, pl.ds(row + at + p * part, height), :], back_turn, 1
                        )
                        for b in range(side_blocks + 1)
                    ]
                    cuts.append(
                        [jnp.where(keep, turned[b], turned[b + 1]) for b in range(side_blocks)]
                    )
                blocks = []
                for b in range(side_blocks):
                    cols = slice(b * LANES, (b + 1) * LANES)
                    probe_re = probe_ref[0, pl.ds(at + p * part, height), cols]
                    probe_im = probe_ref[1, pl.ds(at + p * part, height), cols]
                    re, im = cuts[0][b], cuts[1][b]
                    blocks.append((probe_re * re - probe_im * im, probe_re * im + probe_im * re))
                waves.append(blocks)
            for b in range(side_blocks):
                cols = slice(b * LANES, (b + 1) * LANES)
                sums = butterfly([waves[p][b] for p in range(RADIX)], -1)
                for q in range(RADIX):
                    mixed[q, pl.ds(at, height), cols] = sums[q][0].astype(jnp.bfloat16)
                    mixed[q, pl.ds(at + part, height), cols] = sums[q][1].astype(jnp.bfloat16)
            return carry

        lax.fori_loop(0, part // height, load_rows, 0, unroll=part // height)

        for q in range(RADIX):
            half = dot(rows_ref[q], mixed[q])
            parts = [
                (half[:part, p * part : (p + 1) * part], half[part:, p * part : (p + 1) * part])
                for p in range(RADIX)
            ]
            misfits = []
            for other, (re, im) in enumerate(butterfly(parts, -1)):
                far = dot(jnp.concatenate([re, im], axis=1).astype(jnp.bfloat16), cols_ref[other])
                far_re, far_im = far[:, :part], far[:, part:]
                seen = measured_ref[
                    slot, q * part : (q + 1) * part, other * part : (other + 1) * part
                ].astype(jnp.float32)
                misfit = far_re * far_re + far_im * far_im - seen
                misfits.append(
                    jnp.concatenate([misfit * far_re, misfit * far_im], axis=0).astype(jnp.bfloat16)
                )
            spectra[q] = dot(cols_ref[q], jnp.concatenate(misfits, axis=1))

        def mix_rows(i, carry):
            at = pl.multiple_of(i * height, height)
            for other in range(RADIX):
                cols = slice(other * part, (other + 1) * part)
                parts = [
                    (spectra[q, pl.ds(at, height), cols], spectra[q, pl.ds(at + part, height), cols])
                    for q in range(RADIX)
                ]
                for p, (re, im) in enumerate(butterfly(parts, 1)):
                    backs[other, pl.ds(at + p * part, height), :] = jnp.concatenate(
                        [re, im], axis=1
                    ).astype(jnp.bfloat16)
            return carry

        lax.fori_loop(0, part // height, mix_rows, 0, unroll=part // height)

        def add_rows(i, carry):
            tall = 256
            at = pl.multiple_of(i * tall, tall)
            parts = []
            for other in range(RADIX):
                grad = dot(backs[other, pl.ds(at, tall), :], rows_ref[other])
                parts.append((grad[:, :part], grad[:, part:]))
            turned = [[], []]
            for b, (re, im) in enumerate(butterfly(parts, 1)):
                cols = slice(b * part, (b + 1) * part)
                probe_re = probe_ref[0, pl.ds(at, tall), cols]
                probe_im = probe_ref[1, pl.ds(at, tall), cols]
                turned[0].append(pltpu.roll(probe_re * re + probe_im * im, turn, 1))
                turned[1].append(pltpu.roll(probe_re * im - probe_im * re, turn, 1))
            for c in range(2):
                for b in range(side_blocks + 1):
                    if b == 0:
                        value = jnp.where(enter, turned[c][0], 0.0)
                    elif b == side_blocks:
                        value = jnp.where(enter, 0.0, turned[c][b - 1])
                    else:
                        value = jnp.where(enter, turned[c][b], turned[c][b - 1])
                    grown[c, block + b, pl.ds(row + at, tall), :] += value
            return carry

        lax.fori_loop(0, side_len // 256, add_rows, 0)
        return carry

    lax.fori_loop(0, live_ref[0, lax.axis_index("scan")], one_slot, 0)

    stores = [
        pltpu.make_async_copy(
            grown.at[c, b, :tile_len, :],
            out_hbm.at[c, :, b * LANES : (b + 1) * LANES],
            puts.at[3 + c * own_blocks + b],
        )
        for c in range(2)
        for b in range(own_blocks)
    ]
    for store in stores:
        store.start()
    for c in range(2):
        for b in range(side_blocks):
            at = slice(b * LANES, (b + 1) * LANES)
            corner_ref[c, :, at] = grown[c, own_blocks + b, tile_len:, :].astype(jnp.bfloat16)
            right_ref[c, :, at] = grown[c, own_blocks + b, :tile_len, :].astype(jnp.bfloat16)
    stores.append(pltpu.make_async_copy(corner_ref, out_corner_hbm, puts.at[0]))
    stores.append(pltpu.make_async_copy(right_ref, out_right_hbm, puts.at[1]))
    stores[-2].start()
    stores[-1].start()
    for c in range(2):
        for b in range(own_blocks):
            at = slice(b * LANES, (b + 1) * LANES)
            below_ref[c, :, at] = grown[c, b, tile_len:, :].astype(jnp.bfloat16)
    stores.append(pltpu.make_async_copy(below_ref, out_below_hbm, puts.at[2]))
    stores[-1].start()
    for store in stores:
        store.wait()


def solve(live_counts, shifts, own, right, below, corner, probe, measured, tables):
    tile_len = own.shape[1]
    side_len = probe.shape[1]
    blocks = (tile_len + side_len) // LANES
    smem = pl.BlockSpec(memory_space=pltpu.SMEM)
    hbm = pl.BlockSpec(memory_space=pltpu.HBM)
    part = side_len // RADIX
    copies = 2 * (tile_len // LANES)
    return pl.pallas_call(
        solve_kernel,
        out_shape=[
            jax.ShapeDtypeStruct(own.shape, jnp.float32),
            jax.ShapeDtypeStruct(right.shape, jnp.bfloat16),
            jax.ShapeDtypeStruct(below.shape, jnp.bfloat16),
            jax.ShapeDtypeStruct(corner.shape, jnp.bfloat16),
        ],
        in_specs=[smem, smem] + [hbm] * 8,
        out_specs=[hbm] * 4,
        scratch_shapes=[
            pltpu.VMEM((2, blocks, tile_len + side_len, LANES), jnp.float32),
            pltpu.VMEM((2, blocks, tile_len + side_len, LANES), jnp.float32),
            pltpu.VMEM((RADIX, 2 * part, side_len), jnp.bfloat16),
            pltpu.VMEM((RADIX, 2 * part, side_len), jnp.float32),
            pltpu.VMEM((RADIX, side_len, 2 * part), jnp.bfloat16),
            pltpu.VMEM(right.shape, jnp.bfloat16),
            pltpu.VMEM(below.shape, jnp.bfloat16),
            pltpu.VMEM(corner.shape, jnp.bfloat16),
            pltpu.VMEM(probe.shape, jnp.float32),
            pltpu.VMEM(measured.shape, jnp.bfloat16),
            pltpu.VMEM(tables[0].shape, jnp.bfloat16),
            pltpu.VMEM(tables[1].shape, jnp.bfloat16),
            pltpu.SemaphoreType.DMA((7 + copies,)),
            pltpu.SemaphoreType.DMA((3 + copies,)),
        ],
        compiler_params=pltpu.CompilerParams(vmem_limit_bytes=vmem_bytes),
    )(live_counts, shifts, own, right, below, corner, probe, measured, *tables)


def shards(axes, object_slab, probe_field, intensities, offsets, live_count):
    right, below, corner, measured = gather(axes, object_slab, intensities[0, 0])
    tables = residue_tables(probe_field.shape[-1])
    own, spill, dropped, both = solve(
        live_count.T, offsets[0, 0].T, object_slab, right, below, corner, probe_field, measured, tables
    )
    return scatter(axes, own, spill, dropped, both)


def solution(mesh):
    placed = (
        P(None, "tile", "scan"),
        P(),
        P("scan", "tile", None, None, None),
        P("scan", "tile", None, None),
        P(None, "tile"),
    )
    axes = tuple((name, mesh.shape[name]) for name in ("scan", "tile"))
    return jax.shard_map(
        functools.partial(shards, axes), mesh=mesh, in_specs=placed, out_specs=P(None, "tile", "scan"), check_vma=False
    )
```

```python
import functools
import math

import jax
import jax.numpy as jnp
import numpy as np
from jax import lax
from jax.experimental import pallas as pl
from jax.experimental.pallas import tpu as pltpu
from jax.sharding import PartitionSpec as P

RADIX = 4
LANES = 128
vmem_bytes = 67043328


def residue_tables(side_len):
    part = side_len // RADIX
    freq = np.arange(side_len).reshape(part, RADIX).T
    across = np.arange(part)
    phase = (freq[:, :, None] * across[None, None, :] % side_len) * (2.0 * math.pi / side_len)
    factor = 1.0 / math.sqrt(side_len)
    cos = np.cos(phase) * factor
    sin = np.sin(phase) * factor
    rows = np.concatenate(
        [np.concatenate([cos, sin], axis=2), np.concatenate([-sin, cos], axis=2)], axis=1
    ).astype(np.float32)
    return jnp.asarray(rows, jnp.bfloat16), jnp.asarray(rows.swapaxes(1, 2), jnp.bfloat16)


def sorted_by_residue(side_len):
    at = np.arange(side_len)
    source = at % (side_len // RADIX) * RADIX + at // (side_len // RADIX)
    sort = (source[:, None] == at[None, :]).astype(np.float32)
    return jnp.asarray(sort, jnp.bfloat16), jnp.asarray(sort.T, jnp.bfloat16)


def dot(a, b):
    return jnp.dot(a, b, preferred_element_type=jnp.float32)


def butterfly(parts, sign):
    (r0, i0), (r1, i1), (r2, i2), (r3, i3) = parts
    ar, ai, br, bi = r0 + r2, i0 + i2, r1 + r3, i1 + i3
    cr, ci, dr, di = r0 - r2, i0 - i2, r1 - r3, i1 - i3
    plus = (cr - di, ci + dr)
    minus = (cr + di, ci - dr)
    first, third = (plus, minus) if sign > 0 else (minus, plus)
    return [(ar + br, ai + bi), first, (ar - br, ai - bi), third]


def neighbours(axes):
    result = []
    for name, count in axes:
        me = lax.axis_index(name)
        result.append((me > 0, {name: me - 1}, me < count - 1, {name: me + 1}))
    return result


def meet(peers):
    barrier = pltpu.get_barrier_semaphore()
    for has_low, low, has_high, high in peers:
        for there, peer in ((has_low, low), (has_high, high)):

            @pl.when(there)
            def _(peer=peer):
                pl.semaphore_signal(
                    barrier, inc=1, device_id=peer, device_id_type=pl.DeviceIdType.MESH
                )

    count = sum(
        there.astype(jnp.int32) for has_low, _, has_high, _ in peers for there in (has_low, has_high)
    )
    pl.semaphore_wait(barrier, count)


def remote(source, target, sends, receives, index, peer):
    return pltpu.make_async_remote_copy(
        src_ref=source,
        dst_ref=target,
        send_sem=sends.at[index],
        recv_sem=receives.at[index],
        device_id=peer,
        device_id_type=pl.DeviceIdType.MESH,
    )


def gather_kernel(
    axes,
    own_hbm,
    measured_hbm,
    sort_hbm,
    unsort_hbm,
    right_hbm,
    below_hbm,
    corner_hbm,
    sorted_hbm,
    own,
    sent,
    right,
    below,
    corner,
    measured,
    arranged,
    sort,
    unsort,
    sends,
    receives,
    fetches,
    puts,
):
    side_len = measured.shape[-1]
    scan, tile = neighbours(axes)
    has_left, left, has_right, _ = scan
    has_up, up, has_down, _ = tile
    first = pltpu.make_async_copy(
        own_hbm.at[:, :side_len, :side_len], own.at[:, :side_len, :side_len], fetches.at[0]
    )
    second = pltpu.make_async_copy(
        own_hbm.at[:, side_len:, :side_len], own.at[:, side_len:, :side_len], fetches.at[1]
    )
    third = pltpu.make_async_copy(
        own_hbm.at[:, :side_len, side_len:], own.at[:, :side_len, side_len:], fetches.at[2]
    )
    fetch_measured = pltpu.make_async_copy(measured_hbm, measured, fetches.at[3])
    fetch_sort = pltpu.make_async_copy(sort_hbm, sort, fetches.at[4])
    fetch_unsort = pltpu.make_async_copy(unsort_hbm, unsort, fetches.at[5])
    first.start()
    second.start()
    third.start()
    fetch_sort.start()
    fetch_unsort.start()
    fetch_measured.start()
    top = remote(
        sent.at[:, :side_len, :side_len], right.at[:, :side_len, :], sends, receives, 0, left
    )
    rest = remote(
        sent.at[:, side_len:, :side_len], right.at[:, side_len:, :], sends, receives, 1, left
    )
    under = remote(sent.at[:, :side_len, :], below, sends, receives, 2, up)
    across = remote(right.at[:, :side_len, :], corner, sends, receives, 3, up)
    first.wait()
    sent[:, :side_len, :side_len] = own[:, :side_len, :side_len].astype(jnp.bfloat16)
    meet((scan, tile))

    @pl.when(has_left)
    def _():
        top.start()

    second.wait()
    third.wait()
    sent[:, side_len:, :side_len] = own[:, side_len:, :side_len].astype(jnp.bfloat16)
    sent[:, :side_len, side_len:] = own[:, :side_len, side_len:].astype(jnp.bfloat16)

    @pl.when(has_left)
    def _():
        rest.start()

    @pl.when(has_up)
    def _():
        under.start()

    @pl.when(jnp.logical_not(has_right))
    def _():
        right[...] = jnp.zeros_like(right)

    @pl.when(jnp.logical_not(has_down))
    def _():
        below[...] = jnp.zeros_like(below)
        corner[...] = jnp.zeros_like(corner)

    fetch_sort.wait()
    fetch_unsort.wait()
    fetch_measured.wait()

    def sort_slot(slot, carry):
        rows = dot(sort[...], measured[slot]).astype(jnp.bfloat16)
        arranged[slot] = dot(rows, unsort[...]).astype(jnp.bfloat16)
        return carry

    lax.fori_loop(0, measured.shape[0], sort_slot, 0)
    put_sorted = pltpu.make_async_copy(arranged, sorted_hbm, puts.at[0])
    put_sorted.start()

    @pl.when(has_right)
    def _():
        top.wait_recv()

    @pl.when(has_up)
    def _():
        across.start()

    put_top = pltpu.make_async_copy(
        right.at[:, :side_len, :], right_hbm.at[:, :side_len, :], puts.at[1]
    )
    put_top.start()

    @pl.when(has_down)
    def _():
        under.wait_recv()

    put_below = pltpu.make_async_copy(below, below_hbm, puts.at[2])
    put_below.start()

    @pl.when(has_right)
    def _():
        rest.wait_recv()

    put_rest = pltpu.make_async_copy(
        right.at[:, side_len:, :], right_hbm.at[:, side_len:, :], puts.at[3]
    )
    put_rest.start()

    @pl.when(has_down)
    def _():
        across.wait_recv()

    put_corner = pltpu.make_async_copy(corner, corner_hbm, puts.at[4])
    put_corner.start()

    @pl.when(has_left)
    def _():
        top.wait_send()
        rest.wait_send()

    @pl.when(has_up)
    def _():
        under.wait_send()
        across.wait_send()

    put_sorted.wait()
    put_top.wait()
    put_below.wait()
    put_rest.wait()
    put_corner.wait()


def gather(axes, own, measured):
    side_len = measured.shape[-1]
    tile_len = own.shape[1]
    hbm = pl.BlockSpec(memory_space=pltpu.HBM)
    right = (2, tile_len, side_len)
    below = (2, side_len, tile_len)
    corner = (2, side_len, side_len)
    return pl.pallas_call(
        functools.partial(gather_kernel, axes),
        out_shape=[
            jax.ShapeDtypeStruct(shape, jnp.bfloat16)
            for shape in (right, below, corner, measured.shape)
        ],
        in_specs=[hbm] * 4,
        out_specs=[hbm] * 4,
        scratch_shapes=[
            pltpu.VMEM(own.shape, jnp.float32),
            pltpu.VMEM(own.shape, jnp.bfloat16),
            pltpu.VMEM(right, jnp.bfloat16),
            pltpu.VMEM(below, jnp.bfloat16),
            pltpu.VMEM(corner, jnp.bfloat16),
            pltpu.VMEM(measured.shape, jnp.bfloat16),
            pltpu.VMEM(measured.shape, jnp.bfloat16),
            pltpu.VMEM((side_len, side_len), jnp.bfloat16),
            pltpu.VMEM((side_len, side_len), jnp.bfloat16),
            pltpu.SemaphoreType.DMA((4,)),
            pltpu.SemaphoreType.DMA((4,)),
            pltpu.SemaphoreType.DMA((6,)),
            pltpu.SemaphoreType.DMA((5,)),
        ],
        compiler_params=pltpu.CompilerParams(
            collective_id=0, has_side_effects=True, vmem_limit_bytes=vmem_bytes
        ),
    )(own, measured, *sorted_by_residue(side_len))


def scatter_kernel(
    axes,
    own_hbm,
    spill_hbm,
    drop_hbm,
    both_hbm,
    total,
    spill,
    joined,
    landed,
    from_left,
    from_up,
    sends,
    receives,
    fetches,
):
    side_len = landed.shape[1]
    scan, tile = neighbours(axes)
    has_left, _, has_right, right = scan
    has_up, _, has_down, down = tile
    fetch_spill = pltpu.make_async_copy(spill_hbm.at[:, :side_len, :], spill, fetches.at[0])
    fetch_own = pltpu.make_async_copy(own_hbm, total, fetches.at[1])
    fetch_spill.start()
    fetch_own.start()
    meet((scan, tile))
    corner = remote(both_hbm, landed, sends, receives, 0, down)
    under = remote(drop_hbm, from_up, sends, receives, 1, down)
    rest = remote(
        spill_hbm.at[:, side_len:, :], from_left.at[:, side_len:, :], sends, receives, 2, right
    )
    top = remote(joined, from_left.at[:, :side_len, :], sends, receives, 3, right)

    @pl.when(has_down)
    def _():
        corner.start()

    @pl.when(has_right)
    def _():
        rest.start()

    @pl.when(has_down)
    def _():
        under.start()

    @pl.when(jnp.logical_not(has_up))
    def _():
        landed[...] = jnp.zeros_like(landed)

    fetch_spill.wait()

    @pl.when(has_up)
    def _():
        corner.wait_recv()

    joined[...] = (spill[...].astype(jnp.float32) + landed[...].astype(jnp.float32)).astype(
        jnp.bfloat16
    )

    @pl.when(has_right)
    def _():
        top.start()

    fetch_own.wait()

    @pl.when(has_left)
    def _():
        rest.wait_recv()
        total[:, side_len:, :side_len] += from_left[:, side_len:, :].astype(jnp.float32)

    @pl.when(has_up)
    def _():
        under.wait_recv()
        total[:, :side_len, :] += from_up[...].astype(jnp.float32)

    @pl.when(has_left)
    def _():
        top.wait_recv()
        total[:, :side_len, :side_len] += from_left[:, :side_len, :].astype(jnp.float32)

    @pl.when(has_right)
    def _():
        rest.wait_send()
        top.wait_send()

    @pl.when(has_down)
    def _():
        corner.wait_send()
        under.wait_send()


def scatter(axes, own, spill, dropped, both):
    hbm = pl.BlockSpec(memory_space=pltpu.HBM)
    return pl.pallas_call(
        functools.partial(scatter_kernel, axes),
        out_shape=pltpu.VMEM(own.shape, jnp.float32),
        in_specs=[hbm] * 4,
        out_specs=pl.BlockSpec(memory_space=pltpu.VMEM),
        scratch_shapes=[
            pltpu.VMEM(both.shape, jnp.bfloat16),
            pltpu.VMEM(both.shape, jnp.bfloat16),
            pltpu.VMEM(both.shape, jnp.bfloat16),
            pltpu.VMEM(spill.shape, jnp.bfloat16),
            pltpu.VMEM(dropped.shape, jnp.bfloat16),
            pltpu.SemaphoreType.DMA((4,)),
            pltpu.SemaphoreType.DMA((4,)),
            pltpu.SemaphoreType.DMA((2,)),
        ],
        compiler_params=pltpu.CompilerParams(
            collective_id=1, has_side_effects=True, vmem_limit_bytes=vmem_bytes - own.size * 4 - (1 << 20)
        ),
    )(own, spill, dropped, both)


def solve_kernel(
    live_ref,
    shift_ref,
    own_hbm,
    right_hbm,
    below_hbm,
    corner_hbm,
    probe_hbm,
    measured_hbm,
    rows_hbm,
    cols_hbm,
    out_hbm,
    out_right_hbm,
    out_below_hbm,
    out_corner_hbm,
    field,
    grown,
    mixed,
    spectra,
    backs,
    right_ref,
    below_ref,
    corner_ref,
    probe_ref,
    measured_ref,
    rows_ref,
    cols_ref,
    fetches,
    puts,
):
    tile_len = own_hbm.shape[1]
    side_len = probe_ref.shape[1]
    part = side_len // RADIX
    own_blocks = tile_len // LANES
    side_blocks = side_len // LANES
    lane = lax.broadcasted_iota(jnp.int32, (1, LANES), 1)

    loads = [
        pltpu.make_async_copy(source, target, fetches.at[i])
        for i, (source, target) in enumerate(
            (
                (below_hbm, below_ref),
                (right_hbm, right_ref),
                (corner_hbm, corner_ref),
                (probe_hbm, probe_ref),
                (rows_hbm, rows_ref),
                (cols_hbm, cols_ref),
                (measured_hbm, measured_ref),
            )
        )
    ]
    for load in loads[:3]:
        load.start()
    pieces = [
        pltpu.make_async_copy(
            own_hbm.at[c, :, b * LANES : (b + 1) * LANES],
            field.at[c, b, :tile_len, :],
            fetches.at[len(loads) + c * own_blocks + b],
        )
        for c in range(2)
        for b in range(own_blocks)
    ]
    for load in pieces + loads[3:]:
        load.start()
    grown[...] = jnp.zeros_like(grown)
    loads[0].wait()
    for c in range(2):
        for b in range(own_blocks):
            at = slice(b * LANES, (b + 1) * LANES)
            field[c, b, tile_len:, :] = below_ref[c, :, at].astype(jnp.float32)
    loads[1].wait()
    loads[2].wait()
    for c in range(2):
        for b in range(side_blocks):
            at = slice(b * LANES, (b + 1) * LANES)
            field[c, own_blocks + b, :tile_len, :] = right_ref[c, :, at].astype(jnp.float32)
            field[c, own_blocks + b, tile_len:, :] = corner_ref[c, :, at].astype(jnp.float32)
    for load in pieces + loads[3:]:
        load.wait()

    def one_slot(slot, carry):
        row = shift_ref[0, slot]
        col = shift_ref[1, slot]
        block = lax.div(col, LANES)
        turn = lax.rem(col, LANES)
        back_turn = lax.rem(LANES - turn, LANES)
        keep = lane < LANES - turn
        enter = lane >= turn
        height = 16

        def load_rows(i, carry):
            at = pl.multiple_of(i * height, height)
            waves = []
            for p in range(RADIX):
                cuts = []
                for c in range(2):
                    turned = [
                        pltpu.roll(
                            field[c, block + b, pl.ds(row + at + p * part, height), :], back_turn, 1
                        )
                        for b in range(side_blocks + 1)
                    ]
                    cuts.append(
                        [jnp.where(keep, turned[b], turned[b + 1]) for b in range(side_blocks)]
                    )
                blocks = []
                for b in range(side_blocks):
                    cols = slice(b * LANES, (b + 1) * LANES)
                    probe_re = probe_ref[0, pl.ds(at + p * part, height), cols]
                    probe_im = probe_ref[1, pl.ds(at + p * part, height), cols]
                    re, im = cuts[0][b], cuts[1][b]
                    blocks.append((probe_re * re - probe_im * im, probe_re * im + probe_im * re))
                waves.append(blocks)
            for b in range(side_blocks):
                cols = slice(b * LANES, (b + 1) * LANES)
                sums = butterfly([waves[p][b] for p in range(RADIX)], -1)
                for q in range(RADIX):
                    mixed[q, pl.ds(at, height), cols] = sums[q][0].astype(jnp.bfloat16)
                    mixed[q, pl.ds(at + part, height), cols] = sums[q][1].astype(jnp.bfloat16)
            return carry

        lax.fori_loop(0, part // height, load_rows, 0, unroll=part // height)

        for q in range(RADIX):
            half = dot(rows_ref[q], mixed[q])
            parts = [
                (half[:part, p * part : (p + 1) * part], half[part:, p * part : (p + 1) * part])
                for p in range(RADIX)
            ]
            misfits = []
            for other, (re, im) in enumerate(butterfly(parts, -1)):
                far = dot(jnp.concatenate([re, im], axis=1).astype(jnp.bfloat16), cols_ref[other])
                far_re, far_im = far[:, :part], far[:, part:]
                seen = measured_ref[
                    slot, q * part : (q + 1) * part, other * part : (other + 1) * part
                ].astype(jnp.float32)
                misfit = far_re * far_re + far_im * far_im - seen
                misfits.append(
                    jnp.concatenate([misfit * far_re, misfit * far_im], axis=0).astype(jnp.bfloat16)
                )
            spectra[q] = dot(cols_ref[q], jnp.concatenate(misfits, axis=1))

        def mix_rows(i, carry):
            at = pl.multiple_of(i * height, height)
            for other in range(RADIX):
                cols = slice(other * part, (other + 1) * part)
                parts = [
                    (spectra[q, pl.ds(at, height), cols], spectra[q, pl.ds(at + part, height), cols])
                    for q in range(RADIX)
                ]
                for p, (re, im) in enumerate(butterfly(parts, 1)):
                    backs[other, pl.ds(at + p * part, height), :] = jnp.concatenate(
                        [re, im], axis=1
                    ).astype(jnp.bfloat16)
            return carry

        lax.fori_loop(0, part // height, mix_rows, 0, unroll=part // height)

        def add_rows(i, carry):
            tall = 256
            at = pl.multiple_of(i * tall, tall)
            parts = []
            for other in range(RADIX):
                grad = dot(backs[other, pl.ds(at, tall), :], rows_ref[other])
                parts.append((grad[:, :part], grad[:, part:]))
            turned = [[], []]
            for b, (re, im) in enumerate(butterfly(parts, 1)):
                cols = slice(b * part, (b + 1) * part)
                probe_re = probe_ref[0, pl.ds(at, tall), cols]
                probe_im = probe_ref[1, pl.ds(at, tall), cols]
                turned[0].append(pltpu.roll(probe_re * re + probe_im * im, turn, 1))
                turned[1].append(pltpu.roll(probe_re * im - probe_im * re, turn, 1))
            for c in range(2):
                for b in range(side_blocks + 1):
                    if b == 0:
                        value = jnp.where(enter, turned[c][0], 0.0)
                    elif b == side_blocks:
                        value = jnp.where(enter, 0.0, turned[c][b - 1])
                    else:
                        value = jnp.where(enter, turned[c][b], turned[c][b - 1])
                    grown[c, block + b, pl.ds(row + at, tall), :] += value
            return carry

        lax.fori_loop(0, side_len // 256, add_rows, 0)
        return carry

    lax.fori_loop(0, live_ref[0, lax.axis_index("scan")], one_slot, 0)

    stores = [
        pltpu.make_async_copy(
            grown.at[c, b, :tile_len, :],
            out_hbm.at[c, :, b * LANES : (b + 1) * LANES],
            puts.at[3 + c * own_blocks + b],
        )
        for c in range(2)
        for b in range(own_blocks)
    ]
    for store in stores:
        store.start()
    for c in range(2):
        for b in range(side_blocks):
            at = slice(b * LANES, (b + 1) * LANES)
            corner_ref[c, :, at] = grown[c, own_blocks + b, tile_len:, :].astype(jnp.bfloat16)
            right_ref[c, :, at] = grown[c, own_blocks + b, :tile_len, :].astype(jnp.bfloat16)
    stores.append(pltpu.make_async_copy(corner_ref, out_corner_hbm, puts.at[0]))
    stores.append(pltpu.make_async_copy(right_ref, out_right_hbm, puts.at[1]))
    stores[-2].start()
    stores[-1].start()
    for c in range(2):
        for b in range(own_blocks):
            at = slice(b * LANES, (b + 1) * LANES)
            below_ref[c, :, at] = grown[c, b, tile_len:, :].astype(jnp.bfloat16)
    stores.append(pltpu.make_async_copy(below_ref, out_below_hbm, puts.at[2]))
    stores[-1].start()
    for store in stores:
        store.wait()


def solve(live_counts, shifts, own, right, below, corner, probe, measured, tables):
    tile_len = own.shape[1]
    side_len = probe.shape[1]
    blocks = (tile_len + side_len) // LANES
    smem = pl.BlockSpec(memory_space=pltpu.SMEM)
    hbm = pl.BlockSpec(memory_space=pltpu.HBM)
    part = side_len // RADIX
    copies = 2 * (tile_len // LANES)
    return pl.pallas_call(
        solve_kernel,
        out_shape=[
            jax.ShapeDtypeStruct(own.shape, jnp.float32),
            jax.ShapeDtypeStruct(right.shape, jnp.bfloat16),
            jax.ShapeDtypeStruct(below.shape, jnp.bfloat16),
            jax.ShapeDtypeStruct(corner.shape, jnp.bfloat16),
        ],
        in_specs=[smem, smem] + [hbm] * 8,
        out_specs=[hbm] * 4,
        scratch_shapes=[
            pltpu.VMEM((2, blocks, tile_len + side_len, LANES), jnp.float32),
            pltpu.VMEM((2, blocks, tile_len + side_len, LANES), jnp.float32),
            pltpu.VMEM((RADIX, 2 * part, side_len), jnp.bfloat16),
            pltpu.VMEM((RADIX, 2 * part, side_len), jnp.float32),
            pltpu.VMEM((RADIX, side_len, 2 * part), jnp.bfloat16),
            pltpu.VMEM(right.shape, jnp.bfloat16),
            pltpu.VMEM(below.shape, jnp.bfloat16),
            pltpu.VMEM(corner.shape, jnp.bfloat16),
            pltpu.VMEM(probe.shape, jnp.float32),
            pltpu.VMEM(measured.shape, jnp.bfloat16),
            pltpu.VMEM(tables[0].shape, jnp.bfloat16),
            pltpu.VMEM(tables[1].shape, jnp.bfloat16),
            pltpu.SemaphoreType.DMA((7 + copies,)),
            pltpu.SemaphoreType.DMA((3 + copies,)),
        ],
        compiler_params=pltpu.CompilerParams(vmem_limit_bytes=vmem_bytes),
    )(live_counts, shifts, own, right, below, corner, probe, measured, *tables)


def shards(axes, object_slab, probe_field, intensities, offsets, live_count):
    right, below, corner, measured = gather(axes, object_slab, intensities[0, 0])
    tables = residue_tables(probe_field.shape[-1])
    own, spill, dropped, both = solve(
        live_count.T, offsets[0, 0].T, object_slab, right, below, corner, probe_field, measured, tables
    )
    return scatter(axes, own, spill, dropped, both)


def solution(mesh):
    placed = (
        P(None, "tile", "scan"),
        P(),
        P("scan", "tile", None, None, None),
        P("scan", "tile", None, None),
        P(None, "tile"),
    )
    axes = tuple((name, mesh.shape[name]) for name in ("scan", "tile"))
    return jax.shard_map(
        functools.partial(shards, axes), mesh=mesh, in_specs=placed, out_specs=P(None, "tile", "scan"), check_vma=False
    )
```
